512 devices in a mesh: sub: 64 (over z, y), grp: 8 (over x, core).
Axes of the slice: x: 4, y: 8, z: 8, core: 2. Of those that a mesh axis runs over, the one named last changes fastest.
Arguments:
- applied_loads: float32 [2048, 3, 64, 128], P(('sub', 'grp')), may hold values from -12 to 12
- labels: int32 [2048, 64], P(('sub', 'grp')), may hold values from 0 to 7
- shear_modulus: float32 [8], replicated, may hold values from 0.05 to 0.25
- stiff_ratio: float32 [8], replicated, may hold values from 0.5 to 2
- local_order: int32 [512, 1152], P(('sub', 'grp')), may hold values from 0 to 1151, each once within a row
- local_inverse: bfloat16 [512, 1152, 1152], P(('sub', 'grp')), may hold values from -0.05 to 0.2
- coarse_basis: float32 [512, 4, 1152], P(('sub', 'grp')), may hold values from -0.1875 to 0.1875
- coarse_inverse: float32 [2048, 2048], P('sub'), may hold values from -0.05 to 0.2
Outputs:
- solution: float32 [2048, 3, 64, 128], P(('sub', 'grp'))
- residual: float32 [2048, 3, 64, 128], P(('sub', 'grp'))
- coarse_values: float32 [2048, 128], P(('sub', 'grp'))
The draws below stay inside these ranges and needn't reach their ends.
Inputs may be any that keep to these rules, and one draw needn't show every extreme that they name: `local_order`: every row holds each number from 0 to 1151 once.
All inputs are finite; a program needn't handle non-finite values.
Results may differ from the reference program's by a relative error of at most 0.0015.
Values sent between devices are 32-bit elements; how exact they have to be, the bound alone decides.
A program may use at most 64 MiB of HBM per device.

```python
import math
import jax
import jax.numpy as jnp
from jax import lax

NY = 8
NZ = 8
PLANES = 4
RHS = 128
CV_DEV = 4
ITERS = 3
REGIONS = 8
NODES = 64
SUBN = 1152
NPL = 2048
NC = 2048
DEVICES = 512


def symmetric_draw(key, order, lowest, highest, spread):
    key_diag, key_jitter = jax.random.split(key)
    diagonal = jnp.exp(jax.random.uniform(key_diag, (order,), jnp.float32, math.log(lowest), math.log(highest)))
    jitter = jax.random.normal(key_jitter, (order, order), jnp.float32) * (spread / math.sqrt(order))
    return (jitter + jitter.T) * 0.7071 + jnp.diag(diagonal)


def draw_local_inverse(key, part):
    device_keys = jax.random.split(jax.random.fold_in(key, 11), DEVICES)

    def single(device_key):
        return symmetric_draw(device_key, SUBN, 0.06, 0.12, 0.025).astype(jnp.bfloat16)
    return lax.map(single, device_keys)


def draw_coarse_inverse(key, part):
    return symmetric_draw(jax.random.fold_in(key, 23), NC, 0.08, 0.16, 0.03)


def with_ends(values, key, least, largest):
    place = [jax.random.randint(jax.random.fold_in(key, axis), (), 0, length) for axis, length in enumerate(values.shape)]
    main_axis = values.shape.index(max(values.shape))
    neighbour = place[:main_axis] + [(place[main_axis] + 1) % values.shape[main_axis]] + place[main_axis + 1:]
    return values.at[tuple(place)].set(least).at[tuple(neighbour)].set(largest)


def block_levels(stream_key, extent, shards, low, high):
    factor_of = 1.0
    for axis_at, blocks in shards:
        steps = jax.random.uniform(jax.random.fold_in(jax.random.fold_in(stream_key, 6), axis_at), (blocks,), jnp.float32, low / len(shards), high / len(shards))
        factor_of = factor_of * jnp.repeat(jnp.exp(steps), extent[axis_at] // blocks).reshape((-1,) + (1,) * (len(extent) - 1 - axis_at))
    return factor_of


def bell_draw(rng, dims, scale, bound, cuts=(), kind=jnp.bfloat16):
    loudness = block_levels(rng, dims, cuts, -0.22, 0.18) if cuts else 1.0
    entries = jax.random.normal(rng, dims, jnp.float32) * scale * loudness
    return jnp.minimum(jnp.maximum(entries, -bound), bound).astype(kind)


def setup_inputs(seed: int = 0) -> dict:
    streams_of = jax.random.split(jax.random.key(seed), 9)
    return {
        "applied_loads": bell_draw(streams_of[0], (NPL, 3, NODES, RHS), 2.0, 12.0, ((0, 512),), jnp.float32),
        "labels": with_ends(jax.random.randint(streams_of[1], (NPL, NODES), 0, REGIONS), jax.random.fold_in(streams_of[1], 1), 0, REGIONS - 1).astype(jnp.int32),
        "shear_modulus": jnp.clip(jnp.exp(jax.random.uniform(streams_of[2], (REGIONS,), jnp.float32, math.log(0.05), math.log(0.25))), 0.05, 0.25),
        "stiff_ratio": jnp.clip(jnp.exp(jax.random.uniform(streams_of[3], (REGIONS,), jnp.float32, math.log(0.5), math.log(2.0))), 0.5, 2.0),
        "local_order": jax.vmap(lambda own: jax.random.permutation(own, SUBN))(jax.random.split(streams_of[4], DEVICES)).reshape((DEVICES, SUBN)).astype(jnp.int32),
        "local_inverse": draw_local_inverse(jax.random.fold_in(streams_of[8], 71), 0),
        "coarse_basis": bell_draw(streams_of[6], (DEVICES, CV_DEV, SUBN), SUBN ** -0.5, 0.1875, ((0, 512),), jnp.float32),
        "coarse_inverse": draw_coarse_inverse(jax.random.fold_in(streams_of[8], 71), 0),
    }


RELAXATION = 0.5
PRECISE = lax.Precision.HIGHEST


def shifted(values, shifts):
    window = tuple(slice(1 + offset, values.shape[dimension] - 1 + offset) for dimension, offset in enumerate(shifts))
    return values[window]


def stiffness(displace, shear_ext, normal_ext):
    padded = jnp.pad(displace, ((0, 0), (0, 0), (1, 1), (1, 1), (0, 0)))
    shear_pad = jnp.pad(shear_ext, ((0, 0), (1, 1), (1, 1)))
    normal_pad = jnp.pad(normal_ext, ((0, 0), (1, 1), (1, 1)))
    results = []
    for component in range(3):
        moving = padded[:, component]
        centre = shifted(moving, (0, 0, 0))
        accumulated = jnp.zeros_like(centre)
        for dimension in range(3):
            coefficient = normal_pad if dimension == component else shear_pad
            middle = shifted(coefficient, (0, 0, 0))
            for direction in (-1, 1):
                offsets = tuple(direction if another == dimension else 0 for another in range(3))
                facing = 0.5 * (middle + shifted(coefficient, offsets))
                accumulated = accumulated + facing[..., None] * (centre - shifted(moving, offsets))
        results.append(accumulated)
    return jnp.stack(results, axis=1)


def lookup(labels, shear_modulus, stiff_ratio):
    onehot = (labels[..., None] == jnp.arange(shear_modulus.shape[0], dtype=jnp.int32)).astype(jnp.float32)
    shear_node = jnp.sum(onehot * shear_modulus, axis=-1)
    normal_node = jnp.sum(onehot * (shear_modulus * (2.0 + stiff_ratio)), axis=-1)
    return shear_node, normal_node


def reference(applied_loads, labels, shear_modulus, stiff_ratio, local_order, local_inverse, coarse_basis, coarse_inverse):
    plane_total = applied_loads.shape[0]
    devices = local_inverse.shape[0]
    forces = applied_loads.reshape(plane_total, 3, NY, NZ, RHS)
    shear_node, normal_node = lookup(labels, shear_modulus, stiff_ratio)
    shear_ext = jnp.pad(shear_node.reshape(plane_total, NY, NZ), ((1, 1), (0, 0), (0, 0)))
    normal_ext = jnp.pad(normal_node.reshape(plane_total, NY, NZ), ((1, 1), (0, 0), (0, 0)))
    plane_pad = ((1, 1), (0, 0), (0, 0), (0, 0), (0, 0))

    def operator(displace):
        return stiffness(jnp.pad(displace, plane_pad), shear_ext, normal_ext)

    def solve_single(bundle):
        ordering, inverse, vector, basis_local, values_local = bundle
        local_part = jnp.dot(inverse, vector[ordering], preferred_element_type=jnp.float32)
        spread = jnp.zeros((SUBN, RHS), jnp.float32).at[ordering].set(local_part)
        return spread + jnp.dot(basis_local.T, values_local, precision=PRECISE)

    solution = jnp.zeros_like(forces)
    coarse_values = jnp.zeros((devices * CV_DEV, RHS), jnp.float32)
    for iteration in range(ITERS):
        remaining = forces - operator(solution)
        padded = jnp.pad(remaining, plane_pad)
        middle = padded[1:-1].reshape(devices, PLANES, 3, NY, NZ, RHS)
        left_plane = padded[0:plane_total:PLANES]
        right_plane = padded[PLANES + 1::PLANES]
        windows = jnp.concatenate([left_plane[:, None], middle, right_plane[:, None]], axis=1).reshape(devices, SUBN, RHS)
        coarse_res = jnp.einsum("dkn,dnr->dkr", coarse_basis, windows, precision=PRECISE).reshape(devices * CV_DEV, RHS)
        coarse_values = jnp.dot(coarse_inverse, coarse_res, precision=PRECISE)
        rounded = windows.astype(jnp.bfloat16)
        corrections = lax.map(solve_single, (local_order, local_inverse, rounded, coarse_basis, coarse_values.reshape(devices, CV_DEV, RHS)))
        corrections = corrections.reshape(devices, PLANES + 2, 3, NY, NZ, RHS)
        owned = corrections[:, 1:PLANES + 1]
        owned = owned.at[1:, 0].add(corrections[:-1, PLANES + 1])
        owned = owned.at[:-1, PLANES - 1].add(corrections[1:, 0])
        solution = solution + RELAXATION * owned.reshape(plane_total, 3, NY, NZ, RHS)
    final_residual = forces - operator(solution)
    return (solution.reshape(plane_total, 3, NY * NZ, RHS), final_residual.reshape(plane_total, 3, NY * NZ, RHS), coarse_values)
```

```python
import functools

import jax
import jax.numpy as jnp
from jax import lax
from jax.experimental import pallas as pl
from jax.experimental.pallas import tpu as pltpu
from jax.sharding import PartitionSpec as P

ITERS = 3
NODES = 64
NB = 8
CV = 4
SUBN = 1152
LANES = 128
PLANE = 3 * NODES
MESH = pl.DeviceIdType.MESH
F32 = jnp.float32
BF16 = jnp.bfloat16


def wait_for(ref, sem):
    pltpu.make_async_copy(ref, ref, sem).wait()


def iota(shape, axis):
    return lax.broadcasted_iota(jnp.int32, shape, axis)


def split(x):
    high = x.astype(BF16)
    return high, (x - high.astype(F32)).astype(BF16)


def kernel(
    side,
    groups,
    regions,
    loads,
    labels,
    shear,
    stiff,
    order,
    inverse,
    basis,
    coarse,
    sol_out,
    res_out,
    cv_out,
    res,
    sol,
    zbuf,
    vcat,
    pv,
    ycat,
    yown,
    yleft,
    yright,
    perm,
    permt,
    inv,
    ordv,
    ordt,
    lab,
    bas,
    crs,
    csel,
    cext,
    cbig,
    gone,
    gtwo,
    part,
    arrive,
    table,
    mods,
    off,
    diag,
    xb,
    xbt,
    cols,
    acols,
    mpack,
    apack,
    bam,
    qnext,
    cnow,
    csum,
    load_sem,
    halo_send,
    halo_recv,
    ext_send,
    ext_recv,
    one_send,
    one_recv,
    two_send,
    two_recv,
    thr_send,
    thr_recv,
    y_send,
    y_recv,
    out_sem,
):
    subs = side * side
    chain = subs * groups
    s = lax.axis_index("sub")
    g = lax.axis_index("grp")
    core = lax.rem(g, 2)
    z = lax.div(s, side)
    y = lax.rem(s, side)
    first = (1 - core) * y + core * z
    second = (1 - core) * z + core * y
    here = s * groups + g
    before = lax.rem(here + chain - 1, chain)
    after = lax.rem(here + 1, chain)
    left = {"sub": lax.div(before, groups), "grp": lax.rem(before, groups)}
    right = {"sub": lax.div(after, groups), "grp": lax.rem(after, groups)}
    low_sub = {"sub": lax.rem(s + subs - 1, subs), "grp": g}
    high_sub = {"sub": lax.rem(s + 1, subs), "grp": g}
    m_lo = jnp.where(here == 0, 0.0, 1.0).astype(F32)
    m_hi = jnp.where(here == chain - 1, 0.0, 1.0).astype(F32)

    steps = sorted(range(1, side), key=lambda d: -min(d, side - d))
    gsteps = sorted(range(1, groups), key=lambda d: -min(d, groups - d))

    def first_peer(d):
        o = lax.rem(first + d, side)
        return {"sub": (1 - core) * (z * side + o) + core * (o * side + y), "grp": g}

    def second_peer(d):
        o = lax.rem(second + d, side)
        return {"sub": (1 - core) * (o * side + y) + core * (z * side + o), "grp": g}

    def group_peer(d):
        return lax.rem(g + d, groups)

    def local(src, dst, at):
        return pltpu.make_async_copy(src, dst, load_sem.at[at])

    loading = [
        local(loads, res.at[pl.ds(1, 4)], 0),
        local(basis.at[0], bas.at[1], 1),
        local(order, ordv, 2),
        local(coarse, crs, 3),
        local(labels, lab.at[1], 4),
        local(inverse.at[0], inv, 5),
    ]
    for copy in loading:
        copy.start()

    barrier = pltpu.get_barrier_semaphore()
    peers = [left, right, low_sub, high_sub]
    peers += [first_peer(d) for d in steps] + [second_peer(d) for d in steps]
    peers += [{"sub": s, "grp": group_peer(d)} for d in gsteps]
    for peer in peers:
        pl.semaphore_signal(barrier, inc=1, device_id=peer, device_id_type=MESH)
    pl.semaphore_wait(barrier, len(peers))

    def remote(src, dst, send, recv, peer):
        return pltpu.make_async_remote_copy(
            src_ref=src, dst_ref=dst, send_sem=send, recv_sem=recv, device_id=peer, device_id_type=MESH
        )

    halos = [
        remote(loads.at[3], res.at[0], halo_send.at[0], halo_recv.at[0], right),
        remote(loads.at[0], res.at[5], halo_send.at[1], halo_recv.at[1], left),
        remote(basis.at[0], bas.at[0], halo_send.at[2], halo_recv.at[2], right),
        remote(basis.at[0], bas.at[2], halo_send.at[3], halo_recv.at[3], left),
        remote(labels, lab.at[0], halo_send.at[4], halo_recv.at[4], right),
        remote(labels, lab.at[2], halo_send.at[5], halo_recv.at[5], left),
    ]
    for copy in halos:
        copy.start()

    loading[2].wait()
    ordt[...] = jnp.broadcast_to(ordv[...].astype(F32), (LANES, SUBN)).T

    def numbering(i, carry):
        rows = pl.ds(pl.multiple_of(i * LANES, LANES), LANES)
        hit = iota((LANES, SUBN), 0) + i * LANES == ordv[...]
        permt[rows, :] = jnp.where(hit, 1.0, 0.0).astype(BF16)
        number = ordt[rows, :].astype(jnp.int32)
        for c in range(SUBN // LANES):
            lanes = pl.ds(c * LANES, LANES)
            perm[rows, lanes] = jnp.where(number == iota((LANES, LANES), 1) + c * LANES, 1.0, 0.0).astype(BF16)
        return carry

    lax.fori_loop(0, SUBN // LANES, numbering, 0)

    loading[3].wait()
    width = subs * CV
    place = iota((1, width), 1)
    pos = lax.div(place, CV)
    inner, outer = lax.rem(pos, side), lax.div(pos, side)
    owner = (1 - core) * pos + core * (inner * side + outer)
    wanted = (owner * groups + g) * CV + lax.rem(place, CV)
    span = crs.shape[1]
    choose = jnp.where(iota((span, width), 0) == wanted, 1.0, 0.0).astype(BF16)
    c_hi, c_lo = split(crs[...])
    picked = jnp.dot(c_hi, choose, preferred_element_type=F32) + jnp.dot(c_lo, choose, preferred_element_type=F32)
    own_rows = groups * CV
    csel[...] = picked
    cext[pl.ds(8, own_rows), :] = picked
    edges = [
        remote(csel.at[pl.ds(own_rows - 8, 8)], cext.at[pl.ds(0, 8)], ext_send.at[0], ext_recv.at[0], high_sub),
        remote(csel.at[pl.ds(0, 8)], cext.at[pl.ds(own_rows + 8, 8)], ext_send.at[1], ext_recv.at[1], low_sub),
    ]
    for copy in edges:
        copy.start()

    def restrict():
        for e in range(6):
            high, low = split(res[e].reshape(PLANE, LANES))
            vcat[pl.ds(e * PLANE, PLANE), pl.ds(0, LANES)] = high
            vcat[pl.ds(e * PLANE, PLANE), pl.ds(LANES, LANES)] = low
        b_hi, b_lo = split(bas[1])
        both = jnp.concatenate([b_hi.astype(F32), b_lo.astype(F32), jnp.zeros((8, SUBN), F32)], axis=0).astype(BF16)
        prod = jnp.dot(both, vcat[...], preferred_element_type=F32)
        prod = prod[:, :LANES] + prod[:, LANES:]
        return prod[0:CV] + prod[CV : 2 * CV]

    def send_one(k, q):
        gone[k, first] = q
        for d in steps:
            remote(gone.at[k, first], gone.at[k, first], one_send.at[k], one_recv.at[k], first_peer(d)).start()

    loading[0].wait()
    loading[1].wait()
    halos[0].wait_recv()
    halos[1].wait_recv()
    res[0] = res[0] * m_lo
    res[5] = res[5] * m_hi
    send_one(0, restrict())
    sol[...] = jnp.zeros_like(sol)
    csum[...] = jnp.zeros_like(csum)
    loading[5].wait()

    def stencil(src, o, c):
        u = src[o + 1, c].reshape(NB, NB, LANES)
        tx, tr, tc = [int(c == axis) for axis in range(3)]
        below = jnp.concatenate([u[0:1], u[:-1]], axis=0)
        above = jnp.concatenate([u[1:], u[-1:]], axis=0)
        total = diag[o, c].reshape(NB, NB, LANES) * u
        terms = [
            (tx, 0, src[o, c].reshape(NB, NB, LANES)),
            (tx, 1, src[o + 2, c].reshape(NB, NB, LANES)),
            (tr, 2, below),
            (tr, 3, above),
            (tc, 4, pltpu.roll(u, 1, axis=1)),
            (tc, 5, pltpu.roll(u, NB - 1, axis=1)),
        ]
        for kind, way, value in terms:
            total = total - off[o, kind, way].reshape(NB, NB, LANES) * value
        return total.reshape(NODES, LANES)

    def three_parts(x):
        high = x.astype(BF16).astype(F32)
        low = x - high
        return (high + pltpu.roll(low, 16, axis=1) + pltpu.roll(high, 32, axis=1)).astype(BF16)

    def build():
        loading[4].wait()
        for copy in halos[2:]:
            copy.wait_recv()
        table[...] = jnp.zeros_like(table)
        for slot, rows, at, mask in ((0, (2, 4), 0, m_lo), (1, (0, 4), 2, None), (2, (0, 2), 6, m_hi)):
            kinds = lab[slot]
            mu = jnp.zeros(kinds.shape, F32)
            pm = jnp.zeros(kinds.shape, F32)
            for r in range(regions):
                mu = jnp.where(kinds == r, shear[r], mu)
                pm = jnp.where(kinds == r, shear[r] * (2.0 + stiff[r]), pm)
            if mask is not None:
                mu, pm = mu * mask, pm * mask
            count = rows[1] - rows[0]
            table[at : at + count, 0:NODES] = mu[rows[0] : rows[1]]
            table[8 + at : 8 + at + count, 0:NODES] = pm[rows[0] : rows[1]]
        turned = table[...].T
        for e in range(8):
            for kind in range(2):
                at = kind * 8 + e
                mods[kind, e] = jnp.broadcast_to(turned[0:NODES, at : at + 1], (NODES, LANES))

        def coefficients(o, carry):
            m_o = jnp.where(o == 0, m_lo, jnp.where(o == 5, m_hi, 1.0))
            m_down = jnp.where(o <= 1, m_lo, m_o)
            m_up = jnp.where(o >= 4, m_hi, m_o)
            row = iota((NB, NB, LANES), 0)
            col = iota((NB, NB, LANES), 1)
            nothing = jnp.zeros((1, NB, LANES), F32)
            sums = []
            for kind in range(2):
                mid = mods[kind, o + 1].reshape(NB, NB, LANES)
                down = 0.25 * (mid + mods[kind, o].reshape(NB, NB, LANES))
                up = 0.25 * (mid + mods[kind, o + 2].reshape(NB, NB, LANES))
                rm = 0.25 * (mid + jnp.concatenate([nothing, mid[:-1]], axis=0))
                rp = 0.25 * (mid + jnp.concatenate([mid[1:], nothing], axis=0))
                cm = 0.25 * (mid + jnp.where(col == 0, 0.0, pltpu.roll(mid, 1, axis=1)))
                cp = 0.25 * (mid + jnp.where(col == NB - 1, 0.0, pltpu.roll(mid, NB - 1, axis=1)))
                sums.append((down + up, rm + rp, cm + cp))
                parts = (
                    down * m_down,
                    up * m_up,
                    jnp.where(row == 0, 0.0, rm) * m_o,
                    jnp.where(row == NB - 1, 0.0, rp) * m_o,
                    jnp.where(col == 0, 0.0, cm) * m_o,
                    jnp.where(col == NB - 1, 0.0, cp) * m_o,
                )
                for way, value in enumerate(parts):
                    off[o, kind, way] = value.reshape(NODES, LANES)
            for c in range(3):
                total = sums[int(c == 0)][0] + sums[int(c == 1)][1] + sums[int(c == 2)][2]
                diag[o, c] = (total * m_o).reshape(NODES, LANES)
            return carry

        lax.fori_loop(0, 6, coefficients, 0)

        xb[...] = jnp.zeros_like(xb)
        xb[0:CV, :] = bas[0] * m_lo
        xb[CV : 2 * CV, :] = bas[1]
        xb[2 * CV : 3 * CV, :] = bas[2] * m_hi
        for c in range(SUBN // LANES):
            xbt[pl.ds(c * LANES, LANES), :] = xb[:, pl.ds(c * LANES, LANES)].T
        lane = lax.div(iota((PLANE, LANES), 1), CV)
        for e in range(8):
            total = jnp.zeros((PLANE, LANES), F32)
            for which, at in ((0, e + 3), (1, e - 1), (2, e - 5)):
                if 0 <= at < 6:
                    total = total + jnp.where(lane == which, xbt[pl.ds(at * PLANE, PLANE), :], 0.0)
            cols[e] = total.reshape(3, NODES, LANES)
            if 2 <= e < 6:
                mpack[pl.ds((e - 2) * PLANE, PLANE), :] = three_parts(total)

        def on_columns(o, carry):
            rows = pl.multiple_of(o * PLANE, PLANE)
            for c in range(3):
                acols[pl.ds(rows + c * NODES, NODES), :] = stencil(cols, o, c)
            apack[pl.ds(rows, PLANE), :] = three_parts(acols[pl.ds(rows, PLANE), :])
            return carry

        lax.fori_loop(0, 6, on_columns, 0)
        a_hi, a_lo = split(acols[...])
        b_hi, b_lo = split(bas[1])
        both = jnp.concatenate([b_hi.astype(F32), b_lo.astype(F32), jnp.zeros((8, SUBN), F32)], axis=0).astype(BF16)
        prod = jnp.dot(both, a_hi, preferred_element_type=F32) + jnp.dot(both, a_lo, preferred_element_type=F32)
        prod = prod[0:CV] + prod[CV : 2 * CV]
        for i in range(3 * CV):
            bam[i] = jnp.broadcast_to(prod[:, i : i + 1], (CV, LANES))
        cnow[...] = jnp.zeros_like(cnow)

        for copy in edges:
            copy.wait_recv()
        r = iota((groups * 16, own_rows + 16), 0)
        inside = lax.rem(r, 16)
        source = CV + CV * lax.div(r, 16) + inside
        take = jnp.where((iota((groups * 16, own_rows + 16), 1) == source) & (inside < 3 * CV), 1.0, 0.0).astype(BF16)
        e_hi, e_lo = split(cext[...])
        w_hi = jnp.dot(take, e_hi, preferred_element_type=F32).astype(BF16)
        w_lo = jnp.dot(take, e_lo, preferred_element_type=F32).astype(BF16)
        cbig[:, pl.ds(0, width)] = w_hi
        cbig[:, pl.ds(width, width)] = w_lo
        cbig[:, pl.ds(2 * width, width)] = w_hi

    def spread(c):
        c_hi = c.astype(BF16)
        c_lo = (c - c_hi.astype(F32)).astype(BF16)
        return jnp.concatenate([c_hi, c_hi, c_lo, jnp.zeros((LANES - 48, LANES), BF16)], axis=0)

    third = SUBN // 3

    def iteration(k, carry):
        for e in range(6):
            vcat[pl.ds(e * PLANE, PLANE), pl.ds(0, LANES)] = res[e].reshape(PLANE, LANES).astype(BF16)

        def to_local(i, carry):
            rows = pl.ds(pl.multiple_of(i * third, third), third)
            pv[rows, :] = jnp.dot(perm[rows, :], vcat[:, pl.ds(0, LANES)], preferred_element_type=F32).astype(BF16)
            return carry

        lax.fori_loop(0, 3, to_local, 0)

        def solve(i, carry):
            rows = pl.ds(pl.multiple_of(i * third, third), third)
            high, low = split(jnp.dot(inv[rows, :], pv[...], preferred_element_type=F32))
            ycat[rows, pl.ds(0, LANES)] = high
            ycat[rows, pl.ds(LANES, LANES)] = low
            return carry

        lax.fori_loop(0, 3, solve, 0)

        def from_local(i, carry):
            rows = pl.ds(pl.multiple_of(i * third, third), third)
            back = jnp.dot(permt[rows, :], ycat[...], preferred_element_type=F32)
            back = back[:, :LANES] + back[:, LANES:]
            yown[k, pl.ds(2 * i, 2)] = back.reshape(2, 3, NODES, LANES)
            return carry

        lax.fori_loop(0, 3, from_local, 0)
        remote(yown.at[k, pl.ds(3, 3)], yleft.at[k], y_send.at[0, k], y_recv.at[0, k], right).start()
        remote(yown.at[k, pl.ds(0, 3)], yright.at[k], y_send.at[1, k], y_recv.at[1, k], left).start()

        wait_for(gone.at[k, pl.ds(0, side - 1)], one_recv.at[k])
        for d in steps:
            remote(gone.at[k], gtwo.at[k, second], two_send.at[k], two_recv.at[k], second_peer(d)).start()
        gtwo[k, second] = gone[k]

        pl.when(k == 0)(build)

        wait_for(gtwo.at[k, pl.ds(0, side - 1)], two_recv.at[k])
        gathered = gtwo[k].reshape(width, LANES)
        q_hi, q_lo = split(gathered)
        mixed = jnp.concatenate([q_hi, q_hi, q_lo], axis=0)
        part[k] = jnp.dot(cbig[...], mixed, preferred_element_type=F32).reshape(groups, 16, LANES)
        for d in gsteps:
            o = group_peer(d)
            remote(part.at[k, o], arrive.at[k, g], thr_send.at[k], thr_recv.at[k], {"sub": s, "grp": o}).start()
        arrive[k, g] = part[k, g]

        wait_for(yleft.at[k], y_recv.at[0, k])
        wait_for(yright.at[k], y_recv.at[1, k])
        zbuf[0] = yleft[k, 0]
        zbuf[1] = yleft[k, 1] + yown[k, 0]
        zbuf[2] = yleft[k, 2] * m_lo + yown[k, 1]
        zbuf[3] = yown[k, 2]
        zbuf[4] = yown[k, 3]
        zbuf[5] = yown[k, 4] + yright[k, 0] * m_hi
        zbuf[6] = yown[k, 5] + yright[k, 1]
        zbuf[7] = yright[k, 2]
        for e in range(4):
            sol[e] = sol[e] + 0.5 * zbuf[e + 2]

        def update(o, carry):
            for c in range(3):
                res[o, c] = res[o, c] - stencil(zbuf, o, c)
            return carry

        lax.fori_loop(0, 6, update, 0)

        @pl.when(k < ITERS - 1)
        def _():
            qnext[...] = restrict()

        wait_for(arrive.at[k, pl.ds(0, groups - 1)], thr_recv.at[k])
        c = jnp.sum(arrive[k], axis=0)
        cnow[...] = c
        csum[...] = csum[...] + c

        @pl.when(k < ITERS - 1)
        def _():
            q = qnext[...]
            for i in range(3 * CV):
                q = q - bam[i] * jnp.broadcast_to(cnow[i : i + 1, :], (CV, LANES))
            send_one(k + 1, q)

        weights = spread(c)
        for e in range(6):
            change = jnp.dot(apack[pl.ds(e * PLANE, PLANE), :], weights, preferred_element_type=F32)
            res[e] = res[e] - change.reshape(3, NODES, LANES)
        return carry

    lax.fori_loop(0, ITERS, iteration, 0)

    weights = spread(csum[...])
    for e in range(4):
        change = jnp.dot(mpack[pl.ds(e * PLANE, PLANE), :], weights, preferred_element_type=F32)
        sol_out[e] = sol[e] + 0.5 * change.reshape(3, NODES, LANES)
        res_out[e] = res[e + 1]
    cv_out[...] = cnow[CV : 2 * CV, :]

    for copy in halos + edges:
        copy.wait_send()
    for k in range(ITERS):
        wait_for(gone.at[k, pl.ds(0, side - 1)], one_send.at[k])
        wait_for(gtwo.at[k, pl.ds(0, side - 1)], two_send.at[k])
        wait_for(arrive.at[k, pl.ds(0, groups - 1)], thr_send.at[k])
        wait_for(yleft.at[k], y_send.at[0, k])
        wait_for(yright.at[k], y_send.at[1, k])


def body(side, groups, loads, labels, shear, stiff, order, inverse, basis, coarse):
    planes = loads.shape[0]
    regions = shear.shape[0]
    span = coarse.shape[1]
    width = side * side * CV
    own_rows = groups * CV
    plane = (3, NODES, LANES)
    dma = pltpu.SemaphoreType.DMA
    anywhere = pl.BlockSpec(memory_space=pl.ANY)
    scalars = pl.BlockSpec(memory_space=pltpu.SMEM)
    inside = pl.BlockSpec(memory_space=pltpu.VMEM)
    scratch = [
        pltpu.VMEM((6, *plane), F32),
        pltpu.VMEM((4, *plane), F32),
        pltpu.VMEM((8, *plane), F32),
        pltpu.VMEM((SUBN, 2 * LANES), BF16),
        pltpu.VMEM((SUBN, LANES), BF16),
        pltpu.VMEM((SUBN, 2 * LANES), BF16),
        pltpu.VMEM((ITERS, 6, *plane), F32),
        pltpu.VMEM((ITERS, 3, *plane), F32),
        pltpu.VMEM((ITERS, 3, *plane), F32),
        pltpu.VMEM((SUBN, SUBN), BF16),
        pltpu.VMEM((SUBN, SUBN), BF16),
        pltpu.VMEM((SUBN, SUBN), BF16),
        pltpu.VMEM((1, SUBN), jnp.int32),
        pltpu.VMEM((SUBN, LANES), F32),
        pltpu.VMEM((3, 4, NODES), jnp.int32),
        pltpu.VMEM((3, CV, SUBN), F32),
        pltpu.VMEM((own_rows, span), F32),
        pltpu.VMEM((own_rows, width), F32),
        pltpu.VMEM((own_rows + 16, width), F32),
        pltpu.VMEM((groups * 16, 3 * width), BF16),
        pltpu.VMEM((ITERS, side, CV, LANES), F32),
        pltpu.VMEM((ITERS, side, side, CV, LANES), F32),
        pltpu.VMEM((ITERS, groups, 16, LANES), F32),
        pltpu.VMEM((ITERS, groups, 16, LANES), F32),
        pltpu.VMEM((LANES, LANES), F32),
        pltpu.VMEM((2, 8, NODES, LANES), F32),
        pltpu.VMEM((6, 2, 6, NODES, LANES), F32),
        pltpu.VMEM((6, *plane), F32),
        pltpu.VMEM((LANES, SUBN), F32),
        pltpu.VMEM((SUBN, LANES), F32),
        pltpu.VMEM((8, *plane), F32),
        pltpu.VMEM((SUBN, LANES), F32),
        pltpu.VMEM((4 * PLANE, LANES), BF16),
        pltpu.VMEM((SUBN, LANES), BF16),
        pltpu.VMEM((3 * CV, CV, LANES), F32),
        pltpu.VMEM((CV, LANES), F32),
        pltpu.VMEM((16, LANES), F32),
        pltpu.VMEM((16, LANES), F32),
        dma((6,)),
        dma((6,)),
        dma((6,)),
        dma((2,)),
        dma((2,)),
        dma((ITERS,)),
        dma((ITERS,)),
        dma((ITERS,)),
        dma((ITERS,)),
        dma((ITERS,)),
        dma((ITERS,)),
        dma((2, ITERS)),
        dma((2, ITERS)),
        dma,
    ]
    return pl.pallas_call(
        functools.partial(kernel, side, groups, regions),
        out_shape=(
            jax.ShapeDtypeStruct((planes, *plane), F32),
            jax.ShapeDtypeStruct((planes, *plane), F32),
            jax.ShapeDtypeStruct((CV, LANES), F32),
        ),
        in_specs=[anywhere, anywhere, scalars, scalars, anywhere, anywhere, anywhere, anywhere],
        out_specs=(inside, inside, inside),
        scratch_shapes=scratch,
        compiler_params=pltpu.CompilerParams(collective_id=0, has_side_effects=True),
        name="schwarz",
    )(loads, labels, shear, stiff, order, inverse, basis, coarse)


def solution(mesh):
    subs, groups = mesh.shape["sub"], mesh.shape["grp"]
    side = round(subs**0.5)
    chain = ("sub", "grp")
    return jax.shard_map(
        functools.partial(body, side, groups),
        mesh=mesh,
        in_specs=(
            P(chain, None, None, None),
            P(chain, None),
            P(),
            P(),
            P(chain, None),
            P(chain, None, None),
            P(chain, None, None),
            P("sub", None),
        ),
        out_specs=(P(chain, None, None, None), P(chain, None, None, None), P(chain, None)),
        check_vma=False,
    )
```

```python
import functools

import jax
import jax.numpy as jnp
from jax import lax
from jax.experimental import pallas as pl
from jax.experimental.pallas import tpu as pltpu
from jax.sharding import PartitionSpec as P

ITERS = 3
NODES = 64
NB = 8
CV = 4
SUBN = 1152
LANES = 128
PLANE = 3 * NODES
MESH = pl.DeviceIdType.MESH
F32 = jnp.float32
BF16 = jnp.bfloat16


def wait_for(ref, sem):
    pltpu.make_async_copy(ref, ref, sem).wait()


def iota(shape, axis):
    return lax.broadcasted_iota(jnp.int32, shape, axis)


def split(x):
    high = x.astype(BF16)
    return high, (x - high.astype(F32)).astype(BF16)


def kernel(
    side,
    groups,
    regions,
    loads,
    labels,
    shear,
    stiff,
    order,
    inverse,
    basis,
    coarse,
    sol_out,
    res_out,
    cv_out,
    res,
    sol,
    zbuf,
    vcat,
    pv,
    ycat,
    yown,
    yleft,
    yright,
    perm,
    permt,
    inv,
    ordv,
    ordt,
    lab,
    bas,
    crs,
    csel,
    cext,
    cbig,
    known,
    part,
    arrive,
    table,
    mods,
    off,
    diag,
    xb,
    xbt,
    cols,
    acols,
    mpack,
    apack,
    bam,
    qnext,
    cnow,
    csum,
    load_sem,
    halo_send,
    halo_recv,
    ext_send,
    ext_recv,
    one_send,
    one_recv,
    thr_send,
    thr_recv,
    y_send,
    y_recv,
):
    subs = side * side
    chain = subs * groups
    s = lax.axis_index("sub")
    g = lax.axis_index("grp")
    z = lax.div(s, side)
    y = lax.rem(s, side)
    here = s * groups + g
    before = lax.rem(here + chain - 1, chain)
    after = lax.rem(here + 1, chain)
    left = {"sub": lax.div(before, groups), "grp": lax.rem(before, groups)}
    right = {"sub": lax.div(after, groups), "grp": lax.rem(after, groups)}
    low_sub = {"sub": lax.rem(s + subs - 1, subs), "grp": g}
    high_sub = {"sub": lax.rem(s + 1, subs), "grp": g}
    m_lo = jnp.where(here == 0, 0.0, 1.0).astype(F32)
    m_hi = jnp.where(here == chain - 1, 0.0, 1.0).astype(F32)

    gsteps = sorted(range(1, groups), key=lambda d: -min(d, groups - d))

    half = side // 2
    skip = half * side + half

    def far_first(i):
        oz = lax.rem(z + half + lax.div(i, side), side)
        oy = lax.rem(y + half + lax.rem(i, side), side)
        return {"sub": oz * side + oy, "grp": g}

    def with_sub(visit):
        def step(i, carry):
            visit(far_first(i))
            return carry

        for i in range(subs):
            if i != skip:
                step(i, 0)

    def group_peer(d):
        return lax.rem(g + d, groups)

    def local(src, dst, at):
        return pltpu.make_async_copy(src, dst, load_sem.at[at])

    loading = [
        local(loads, res.at[pl.ds(1, 4)], 0),
        local(basis.at[0], bas.at[1], 1),
        local(order, ordv, 2),
        local(coarse, crs, 3),
        local(labels, lab.at[1], 4),
        local(inverse.at[0], inv, 5),
    ]
    for copy in loading:
        copy.start()

    barrier = pltpu.get_barrier_semaphore()
    peers = [left, right] + [{"sub": s, "grp": group_peer(d)} for d in gsteps]
    for peer in peers:
        pl.semaphore_signal(barrier, inc=1, device_id=peer, device_id_type=MESH)
    with_sub(lambda peer: pl.semaphore_signal(barrier, inc=1, device_id=peer, device_id_type=MESH))
    pl.semaphore_wait(barrier, len(peers) + subs - 1)

    def remote(src, dst, send, recv, peer):
        return pltpu.make_async_remote_copy(
            src_ref=src, dst_ref=dst, send_sem=send, recv_sem=recv, device_id=peer, device_id_type=MESH
        )

    halos = [
        remote(loads.at[3], res.at[0], halo_send.at[0], halo_recv.at[0], right),
        remote(loads.at[0], res.at[5], halo_send.at[1], halo_recv.at[1], left),
        remote(basis.at[0], bas.at[0], halo_send.at[2], halo_recv.at[2], right),
        remote(basis.at[0], bas.at[2], halo_send.at[3], halo_recv.at[3], left),
        remote(labels, lab.at[0], halo_send.at[4], halo_recv.at[4], right),
        remote(labels, lab.at[2], halo_send.at[5], halo_recv.at[5], left),
    ]
    for copy in halos:
        copy.start()

    loading[3].wait()
    width = subs * CV
    place = iota((1, width), 1)
    wanted = (lax.div(place, CV) * groups + g) * CV + lax.rem(place, CV)
    span = crs.shape[1]
    choose = jnp.where(iota((span, width), 0) == wanted, 1.0, 0.0).astype(BF16)
    c_hi, c_lo = split(crs[...])
    picked = jnp.dot(c_hi, choose, preferred_element_type=F32) + jnp.dot(c_lo, choose, preferred_element_type=F32)
    own_rows = groups * CV
    csel[...] = picked
    cext[pl.ds(8, own_rows), :] = picked
    edges = [
        remote(csel.at[pl.ds(own_rows - 8, 8)], cext.at[pl.ds(0, 8)], ext_send.at[0], ext_recv.at[0], high_sub),
        remote(csel.at[pl.ds(0, 8)], cext.at[pl.ds(own_rows + 8, 8)], ext_send.at[1], ext_recv.at[1], low_sub),
    ]
    for copy in edges:
        copy.start()

    loading[2].wait()
    ordt[...] = jnp.broadcast_to(ordv[...].astype(F32), (LANES, SUBN)).T

    def numbering(i, carry):
        rows = pl.ds(pl.multiple_of(i * LANES, LANES), LANES)
        hit = iota((LANES, SUBN), 0) + i * LANES == ordv[...]
        permt[rows, :] = jnp.where(hit, 1.0, 0.0).astype(BF16)
        number = ordt[rows, :].astype(jnp.int32)
        for c in range(SUBN // LANES):
            lanes = pl.ds(c * LANES, LANES)
            perm[rows, lanes] = jnp.where(number == iota((LANES, LANES), 1) + c * LANES, 1.0, 0.0).astype(BF16)
        return carry

    lax.fori_loop(0, SUBN // LANES, numbering, 0)

    def restrict():
        for e in range(6):
            high, low = split(res[e].reshape(PLANE, LANES))
            vcat[pl.ds(e * PLANE, PLANE), pl.ds(0, LANES)] = high
            vcat[pl.ds(e * PLANE, PLANE), pl.ds(LANES, LANES)] = low
        b_hi, b_lo = split(bas[1])
        both = jnp.concatenate([b_hi.astype(F32), b_lo.astype(F32), jnp.zeros((8, SUBN), F32)], axis=0).astype(BF16)
        prod = jnp.dot(both, vcat[...], preferred_element_type=F32)
        prod = prod[:, :LANES] + prod[:, LANES:]
        return prod[0:CV] + prod[CV : 2 * CV]

    def send_all(k, q):
        known[k, s] = q
        with_sub(lambda peer: remote(known.at[k, s], known.at[k, s], one_send.at[k], one_recv.at[k], peer).start())

    loading[0].wait()
    loading[1].wait()
    halos[0].wait_recv()
    halos[1].wait_recv()
    res[0] = res[0] * m_lo
    res[5] = res[5] * m_hi
    send_all(0, restrict())

    sol[...] = jnp.zeros_like(sol)
    csum[...] = jnp.zeros_like(csum)
    loading[5].wait()

    def stencil(src, o, c):
        u = src[o + 1, c].reshape(NB, NB, LANES)
        tx, tr, tc = [int(c == axis) for axis in range(3)]
        below = jnp.concatenate([u[0:1], u[:-1]], axis=0)
        above = jnp.concatenate([u[1:], u[-1:]], axis=0)
        total = diag[o, c].reshape(NB, NB, LANES) * u
        terms = [
            (tx, 0, src[o, c].reshape(NB, NB, LANES)),
            (tx, 1, src[o + 2, c].reshape(NB, NB, LANES)),
            (tr, 2, below),
            (tr, 3, above),
            (tc, 4, pltpu.roll(u, 1, axis=1)),
            (tc, 5, pltpu.roll(u, NB - 1, axis=1)),
        ]
        for kind, way, value in terms:
            total = total - off[o, kind, way].reshape(NB, NB, LANES) * value
        return total.reshape(NODES, LANES)

    def three_parts(x):
        high = x.astype(BF16).astype(F32)
        low = x - high
        return (high + pltpu.roll(low, 16, axis=1) + pltpu.roll(high, 32, axis=1)).astype(BF16)

    def build():
        loading[4].wait()
        for copy in halos[2:]:
            copy.wait_recv()
        table[...] = jnp.zeros_like(table)
        for slot, rows, at, mask in ((0, (2, 4), 0, m_lo), (1, (0, 4), 2, None), (2, (0, 2), 6, m_hi)):
            kinds = lab[slot]
            mu = jnp.zeros(kinds.shape, F32)
            pm = jnp.zeros(kinds.shape, F32)
            for r in range(regions):
                mu = jnp.where(kinds == r, shear[r], mu)
                pm = jnp.where(kinds == r, shear[r] * (2.0 + stiff[r]), pm)
            if mask is not None:
                mu, pm = mu * mask, pm * mask
            count = rows[1] - rows[0]
            table[at : at + count, 0:NODES] = mu[rows[0] : rows[1]]
            table[8 + at : 8 + at + count, 0:NODES] = pm[rows[0] : rows[1]]
        turned = table[...].T
        for e in range(8):
            for kind in range(2):
                at = kind * 8 + e
                mods[kind, e] = jnp.broadcast_to(turned[0:NODES, at : at + 1], (NODES, LANES))

        def coefficients(o, carry):
            m_o = jnp.where(o == 0, m_lo, jnp.where(o == 5, m_hi, 1.0))
            m_down = jnp.where(o <= 1, m_lo, m_o)
            m_up = jnp.where(o >= 4, m_hi, m_o)
            row = iota((NB, NB, LANES), 0)
            col = iota((NB, NB, LANES), 1)
            nothing = jnp.zeros((1, NB, LANES), F32)
            sums = []
            for kind in range(2):
                mid = mods[kind, o + 1].reshape(NB, NB, LANES)
                down = 0.25 * (mid + mods[kind, o].reshape(NB, NB, LANES))
                up = 0.25 * (mid + mods[kind, o + 2].reshape(NB, NB, LANES))
                rm = 0.25 * (mid + jnp.concatenate([nothing, mid[:-1]], axis=0))
                rp = 0.25 * (mid + jnp.concatenate([mid[1:], nothing], axis=0))
                cm = 0.25 * (mid + jnp.where(col == 0, 0.0, pltpu.roll(mid, 1, axis=1)))
                cp = 0.25 * (mid + jnp.where(col == NB - 1, 0.0, pltpu.roll(mid, NB - 1, axis=1)))
                sums.append((down + up, rm + rp, cm + cp))
                parts = (
                    down * m_down,
                    up * m_up,
                    jnp.where(row == 0, 0.0, rm) * m_o,
                    jnp.where(row == NB - 1, 0.0, rp) * m_o,
                    jnp.where(col == 0, 0.0, cm) * m_o,
                    jnp.where(col == NB - 1, 0.0, cp) * m_o,
                )
                for way, value in enumerate(parts):
                    off[o, kind, way] = value.reshape(NODES, LANES)
            for c in range(3):
                total = sums[int(c == 0)][0] + sums[int(c == 1)][1] + sums[int(c == 2)][2]
                diag[o, c] = (total * m_o).reshape(NODES, LANES)
            return carry

        lax.fori_loop(0, 6, coefficients, 0)

        xb[...] = jnp.zeros_like(xb)
        xb[0:CV, :] = bas[0] * m_lo
        xb[CV : 2 * CV, :] = bas[1]
        xb[2 * CV : 3 * CV, :] = bas[2] * m_hi
        for c in range(SUBN // LANES):
            xbt[pl.ds(c * LANES, LANES), :] = xb[:, pl.ds(c * LANES, LANES)].T
        lane = lax.div(iota((PLANE, LANES), 1), CV)
        for e in range(8):
            total = jnp.zeros((PLANE, LANES), F32)
            for which, at in ((0, e + 3), (1, e - 1), (2, e - 5)):
                if 0 <= at < 6:
                    total = total + jnp.where(lane == which, xbt[pl.ds(at * PLANE, PLANE), :], 0.0)
            cols[e] = total.reshape(3, NODES, LANES)
            if 2 <= e < 6:
                mpack[pl.ds((e - 2) * PLANE, PLANE), :] = three_parts(total)

        def on_columns(o, carry):
            rows = pl.multiple_of(o * PLANE, PLANE)
            for c in range(3):
                acols[pl.ds(rows + c * NODES, NODES), :] = stencil(cols, o, c)
            apack[pl.ds(rows, PLANE), :] = three_parts(acols[pl.ds(rows, PLANE), :])
            return carry

        lax.fori_loop(0, 6, on_columns, 0)
        a_hi, a_lo = split(acols[...])
        b_hi, b_lo = split(bas[1])
        both = jnp.concatenate([b_hi.astype(F32), b_lo.astype(F32), jnp.zeros((8, SUBN), F32)], axis=0).astype(BF16)
        prod = jnp.dot(both, a_hi, preferred_element_type=F32) + jnp.dot(both, a_lo, preferred_element_type=F32)
        prod = prod[0:CV] + prod[CV : 2 * CV]
        for i in range(3 * CV):
            bam[i] = jnp.broadcast_to(prod[:, i : i + 1], (CV, LANES))
        cnow[...] = jnp.zeros_like(cnow)

        for copy in edges:
            copy.wait_recv()
        r = iota((groups * 16, own_rows + 16), 0)
        inside = lax.rem(r, 16)
        source = CV + CV * lax.div(r, 16) + inside
        take = jnp.where((iota((groups * 16, own_rows + 16), 1) == source) & (inside < 3 * CV), 1.0, 0.0).astype(BF16)
        e_hi, e_lo = split(cext[...])
        w_hi = jnp.dot(take, e_hi, preferred_element_type=F32).astype(BF16)
        w_lo = jnp.dot(take, e_lo, preferred_element_type=F32).astype(BF16)
        cbig[:, pl.ds(0, width)] = w_hi
        cbig[:, pl.ds(width, width)] = w_lo
        cbig[:, pl.ds(2 * width, width)] = w_hi

    def spread(c):
        c_hi = c.astype(BF16)
        c_lo = (c - c_hi.astype(F32)).astype(BF16)
        return jnp.concatenate([c_hi, c_hi, c_lo, jnp.zeros((LANES - 48, LANES), BF16)], axis=0)

    third = SUBN // 3

    def swap(k, at, count, there, slot, peer, way):
        remote(
            yown.at[k, pl.ds(at, count)], there.at[k, pl.ds(slot, count)], y_send.at[way, k], y_recv.at[way, k], peer
        ).start()

    def iteration(k, carry):
        for e in range(6):
            vcat[pl.ds(e * PLANE, PLANE), pl.ds(0, LANES)] = res[e].reshape(PLANE, LANES).astype(BF16)

        def to_local(i, carry):
            rows = pl.ds(pl.multiple_of(i * third, third), third)
            pv[rows, :] = jnp.dot(perm[rows, :], vcat[:, pl.ds(0, LANES)], preferred_element_type=F32).astype(BF16)
            return carry

        lax.fori_loop(0, 3, to_local, 0)

        def solve(i, carry):
            rows = pl.ds(pl.multiple_of(i * third, third), third)
            high, low = split(jnp.dot(inv[rows, :], pv[...], preferred_element_type=F32))
            ycat[rows, pl.ds(0, LANES)] = high
            ycat[rows, pl.ds(LANES, LANES)] = low
            return carry

        lax.fori_loop(0, 3, solve, 0)

        def from_local(i):
            rows = pl.ds(i * third, third)
            back = jnp.dot(permt[rows, :], ycat[...], preferred_element_type=F32)
            back = back[:, :LANES] + back[:, LANES:]
            yown[k, pl.ds(2 * i, 2)] = back.reshape(2, 3, NODES, LANES)

        from_local(2)
        swap(k, 4, 2, yleft, 1, right, 0)
        from_local(0)
        swap(k, 0, 2, yright, 0, left, 1)
        from_local(1)
        swap(k, 3, 1, yleft, 0, right, 2)
        swap(k, 2, 1, yright, 2, left, 3)

        pl.when(k == 0)(build)

        wait_for(known.at[k, pl.ds(0, subs - 1)], one_recv.at[k])
        gathered = known[k].reshape(width, LANES)
        q_hi, q_lo = split(gathered)
        mixed = jnp.concatenate([q_hi, q_hi, q_lo], axis=0)
        part[k] = jnp.dot(cbig[...], mixed, preferred_element_type=F32).reshape(groups, 16, LANES)
        for d in gsteps:
            o = group_peer(d)
            remote(part.at[k, o], arrive.at[k, g], thr_send.at[k], thr_recv.at[k], {"sub": s, "grp": o}).start()
        arrive[k, g] = part[k, g]

        wait_for(yleft.at[k, pl.ds(1, 2)], y_recv.at[0, k])
        wait_for(yright.at[k, pl.ds(0, 2)], y_recv.at[1, k])
        wait_for(yleft.at[k, pl.ds(0, 1)], y_recv.at[2, k])
        wait_for(yright.at[k, pl.ds(2, 1)], y_recv.at[3, k])
        zbuf[0] = yleft[k, 0]
        zbuf[1] = yleft[k, 1] + yown[k, 0]
        zbuf[2] = yleft[k, 2] * m_lo + yown[k, 1]
        zbuf[3] = yown[k, 2]
        zbuf[4] = yown[k, 3]
        zbuf[5] = yown[k, 4] + yright[k, 0] * m_hi
        zbuf[6] = yown[k, 5] + yright[k, 1]
        zbuf[7] = yright[k, 2]
        for e in range(4):
            sol[e] = sol[e] + 0.5 * zbuf[e + 2]

        def update(o, carry):
            for c in range(3):
                res[o, c] = res[o, c] - stencil(zbuf, o, c)
            return carry

        lax.fori_loop(0, 6, update, 0)

        @pl.when(k < ITERS - 1)
        def _():
            qnext[...] = restrict()

        wait_for(arrive.at[k, pl.ds(0, groups - 1)], thr_recv.at[k])
        c = jnp.sum(arrive[k], axis=0)
        cnow[...] = c
        csum[...] = csum[...] + c

        @pl.when(k < ITERS - 1)
        def _():
            q = qnext[...]
            for i in range(3 * CV):
                q = q - bam[i] * jnp.broadcast_to(cnow[i : i + 1, :], (CV, LANES))
            send_all(k + 1, q)

        weights = spread(c)
        for e in range(6):
            change = jnp.dot(apack[pl.ds(e * PLANE, PLANE), :], weights, preferred_element_type=F32)
            res[e] = res[e] - change.reshape(3, NODES, LANES)
        return carry

    lax.fori_loop(0, ITERS, iteration, 0)

    weights = spread(csum[...])
    for e in range(4):
        change = jnp.dot(mpack[pl.ds(e * PLANE, PLANE), :], weights, preferred_element_type=F32)
        sol_out[e] = sol[e] + 0.5 * change.reshape(3, NODES, LANES)
        res_out[e] = res[e + 1]
    cv_out[...] = cnow[CV : 2 * CV, :]

    for copy in halos + edges:
        copy.wait_send()
    for k in range(ITERS):
        wait_for(known.at[k, pl.ds(0, subs - 1)], one_send.at[k])
        wait_for(arrive.at[k, pl.ds(0, groups - 1)], thr_send.at[k])
        wait_for(yleft.at[k, pl.ds(1, 2)], y_send.at[0, k])
        wait_for(yright.at[k, pl.ds(0, 2)], y_send.at[1, k])
        wait_for(yleft.at[k, pl.ds(0, 1)], y_send.at[2, k])
        wait_for(yright.at[k, pl.ds(2, 1)], y_send.at[3, k])


def deliver(sol_in, res_in, cv_in, sol_out, res_out, cv_out, sem):
    copies = [
        pltpu.make_async_copy(sol_in, sol_out, sem.at[0]),
        pltpu.make_async_copy(res_in, res_out, sem.at[1]),
        pltpu.make_async_copy(cv_in, cv_out, sem.at[2]),
    ]
    for copy in copies:
        copy.start()
    for copy in copies:
        copy.wait()


def body(side, groups, loads, labels, shear, stiff, order, inverse, basis, coarse):
    planes = loads.shape[0]
    regions = shear.shape[0]
    span = coarse.shape[1]
    width = side * side * CV
    own_rows = groups * CV
    plane = (3, NODES, LANES)
    dma = pltpu.SemaphoreType.DMA
    anywhere = pl.BlockSpec(memory_space=pl.ANY)
    scalars = pl.BlockSpec(memory_space=pltpu.SMEM)
    inside = pl.BlockSpec(memory_space=pltpu.VMEM)
    scratch = [
        pltpu.VMEM((6, *plane), F32),
        pltpu.VMEM((4, *plane), F32),
        pltpu.VMEM((8, *plane), F32),
        pltpu.VMEM((SUBN, 2 * LANES), BF16),
        pltpu.VMEM((SUBN, LANES), BF16),
        pltpu.VMEM((SUBN, 2 * LANES), BF16),
        pltpu.VMEM((ITERS, 6, *plane), F32),
        pltpu.VMEM((ITERS, 3, *plane), F32),
        pltpu.VMEM((ITERS, 3, *plane), F32),
        pltpu.VMEM((SUBN, SUBN), BF16),
        pltpu.VMEM((SUBN, SUBN), BF16),
        pltpu.VMEM((SUBN, SUBN), BF16),
        pltpu.VMEM((1, SUBN), jnp.int32),
        pltpu.VMEM((SUBN, LANES), F32),
        pltpu.VMEM((3, 4, NODES), jnp.int32),
        pltpu.VMEM((3, CV, SUBN), F32),
        pltpu.VMEM((own_rows, span), F32),
        pltpu.VMEM((own_rows, width), F32),
        pltpu.VMEM((own_rows + 16, width), F32),
        pltpu.VMEM((groups * 16, 3 * width), BF16),
        pltpu.VMEM((ITERS, side * side, CV, LANES), F32),
        pltpu.VMEM((ITERS, groups, 16, LANES), F32),
        pltpu.VMEM((ITERS, groups, 16, LANES), F32),
        pltpu.VMEM((LANES, LANES), F32),
        pltpu.VMEM((2, 8, NODES, LANES), F32),
        pltpu.VMEM((6, 2, 6, NODES, LANES), F32),
        pltpu.VMEM((6, *plane), F32),
        pltpu.VMEM((LANES, SUBN), F32),
        pltpu.VMEM((SUBN, LANES), F32),
        pltpu.VMEM((8, *plane), F32),
        pltpu.VMEM((SUBN, LANES), F32),
        pltpu.VMEM((4 * PLANE, LANES), BF16),
        pltpu.VMEM((SUBN, LANES), BF16),
        pltpu.VMEM((3 * CV, CV, LANES), F32),
        pltpu.VMEM((CV, LANES), F32),
        pltpu.VMEM((16, LANES), F32),
        pltpu.VMEM((16, LANES), F32),
        dma((6,)),
        dma((6,)),
        dma((6,)),
        dma((2,)),
        dma((2,)),
        dma((ITERS,)),
        dma((ITERS,)),
        dma((ITERS,)),
        dma((ITERS,)),
        dma((4, ITERS)),
        dma((4, ITERS)),
    ]
    outs = (
        jax.ShapeDtypeStruct((planes, *plane), F32),
        jax.ShapeDtypeStruct((planes, *plane), F32),
        jax.ShapeDtypeStruct((CV, LANES), F32),
    )
    held = pl.pallas_call(
        functools.partial(kernel, side, groups, regions),
        out_shape=(
            pltpu.VMEM((planes, *plane), F32),
            pltpu.VMEM((planes, *plane), F32),
            pltpu.VMEM((CV, LANES), F32),
        ),
        in_specs=[anywhere, anywhere, scalars, scalars, anywhere, anywhere, anywhere, anywhere],
        out_specs=(inside, inside, inside),
        scratch_shapes=scratch,
        compiler_params=pltpu.CompilerParams(collective_id=0, has_side_effects=True),
        name="schwarz",
    )(loads, labels, shear, stiff, order, inverse, basis, coarse)
    return pl.pallas_call(
        deliver,
        out_shape=outs,
        in_specs=[anywhere] * 3,
        out_specs=(anywhere,) * 3,
        scratch_shapes=[dma((3,))],
        compiler_params=pltpu.CompilerParams(vmem_limit_bytes=1 << 20),
        name="deliver",
    )(*held)


def solution(mesh):
    subs, groups = mesh.shape["sub"], mesh.shape["grp"]
    side = round(subs**0.5)
    chain = ("sub", "grp")
    return jax.shard_map(
        functools.partial(body, side, groups),
        mesh=mesh,
        in_specs=(
            P(chain, None, None, None),
            P(chain, None),
            P(),
            P(),
            P(chain, None),
            P(chain, None, None),
            P(chain, None, None),
            P("sub", None),
        ),
        out_specs=(P(chain, None, None, None), P(chain, None, None, None), P(chain, None)),
        check_vma=False,
    )
```

```python
import functools

import jax
import jax.numpy as jnp
from jax import lax
from jax.experimental import pallas as pl
from jax.experimental.pallas import tpu as pltpu
from jax.sharding import PartitionSpec as P

ITERS = 3
NODES = 64
NB = 8
CV = 4
SUBN = 1152
LANES = 128
PLANE = 3 * NODES
MESH = pl.DeviceIdType.MESH
F32 = jnp.float32
BF16 = jnp.bfloat16


def wait_for(ref, sem):
    pltpu.make_async_copy(ref, ref, sem).wait()


def iota(shape, axis):
    return lax.broadcasted_iota(jnp.int32, shape, axis)


def split(x):
    high = x.astype(BF16)
    return high, (x - high.astype(F32)).astype(BF16)


def kernel(
    side,
    groups,
    regions,
    loads,
    labels,
    shear_in,
    stiff_in,
    order,
    inverse,
    basis,
    coarse,
    sol_out,
    res_out,
    cv_out,
    rmat,
    edge,
    shear,
    stiff,
    res,
    sol,
    zbuf,
    vcat,
    pv,
    ycat,
    yown,
    yleft,
    yright,
    perm,
    permt,
    inv,
    ordv,
    ordt,
    lab,
    bas,
    crs,
    csel,
    cext,
    cbig,
    known,
    part,
    arrive,
    table,
    mods,
    off,
    diag,
    xb,
    xbt,
    cols,
    acols,
    mpack,
    apack,
    bam,
    qnext,
    cnow,
    csum,
    load_sem,
    halo_send,
    halo_recv,
    ext_send,
    ext_recv,
    one_send,
    one_recv,
    thr_send,
    thr_recv,
    y_send,
    y_recv,
):
    subs = side * side
    chain = subs * groups
    s = lax.axis_index("sub")
    g = lax.axis_index("grp")
    z = lax.div(s, side)
    y = lax.rem(s, side)
    here = s * groups + g
    before = lax.rem(here + chain - 1, chain)
    after = lax.rem(here + 1, chain)
    left = {"sub": lax.div(before, groups), "grp": lax.rem(before, groups)}
    right = {"sub": lax.div(after, groups), "grp": lax.rem(after, groups)}
    low_sub = {"sub": lax.rem(s + subs - 1, subs), "grp": g}
    high_sub = {"sub": lax.rem(s + 1, subs), "grp": g}
    m_lo = jnp.where(here == 0, 0.0, 1.0).astype(F32)
    m_hi = jnp.where(here == chain - 1, 0.0, 1.0).astype(F32)

    gsteps = sorted(range(1, groups), key=lambda d: -min(d, groups - d))

    half = side // 2
    skip = half * side + half

    def far_first(i):
        oz = lax.rem(z + half + lax.div(i, side), side)
        oy = lax.rem(y + half + lax.rem(i, side), side)
        return {"sub": oz * side + oy, "grp": g}

    def with_sub(visit):
        def step(i, carry):
            visit(far_first(i))
            return carry

        for i in range(subs):
            if i != skip:
                step(i, 0)

    def group_peer(d):
        return lax.rem(g + d, groups)

    def local(src, dst, at):
        return pltpu.make_async_copy(src, dst, load_sem.at[at])

    loading = [
        local(loads, res.at[pl.ds(1, 4)], 0),
        local(basis.at[0], bas.at[1], 1),
        local(order, ordv, 2),
        local(coarse, crs, 3),
        local(labels, lab.at[1], 4),
        local(inverse.at[0], inv, 5),
        local(loads.at[3], edge.at[0], 6),
        local(loads.at[0], edge.at[1], 7),
        local(shear_in, shear, 8),
        local(stiff_in, stiff, 9),
    ]
    for at in (6, 7, 0, 1, 2, 3, 4, 8, 9, 5):
        loading[at].start()

    barrier = pltpu.get_barrier_semaphore()
    peers = [left, right] + [{"sub": s, "grp": group_peer(d)} for d in gsteps]
    for peer in peers:
        pl.semaphore_signal(barrier, inc=1, device_id=peer, device_id_type=MESH)
    with_sub(lambda peer: pl.semaphore_signal(barrier, inc=1, device_id=peer, device_id_type=MESH))
    pl.semaphore_wait(barrier, len(peers) + subs - 1)

    def remote(src, dst, send, recv, peer):
        return pltpu.make_async_remote_copy(
            src_ref=src, dst_ref=dst, send_sem=send, recv_sem=recv, device_id=peer, device_id_type=MESH
        )

    loading[6].wait()
    loading[7].wait()
    halos = [
        remote(edge.at[0], res.at[0], halo_send.at[0], halo_recv.at[0], right),
        remote(edge.at[1], res.at[5], halo_send.at[1], halo_recv.at[1], left),
        remote(basis.at[0], bas.at[0], halo_send.at[2], halo_recv.at[2], right),
        remote(basis.at[0], bas.at[2], halo_send.at[3], halo_recv.at[3], left),
        remote(labels, lab.at[0], halo_send.at[4], halo_recv.at[4], right),
        remote(labels, lab.at[2], halo_send.at[5], halo_recv.at[5], left),
    ]
    for copy in halos:
        copy.start()

    loading[3].wait()
    width = subs * CV
    place = iota((1, width), 1)
    wanted = (lax.div(place, CV) * groups + g) * CV + lax.rem(place, CV)
    span = crs.shape[1]
    choose = jnp.where(iota((span, width), 0) == wanted, 1.0, 0.0).astype(BF16)
    c_hi, c_lo = split(crs[...])
    picked = jnp.dot(c_hi, choose, preferred_element_type=F32) + jnp.dot(c_lo, choose, preferred_element_type=F32)
    own_rows = groups * CV
    csel[...] = picked
    cext[pl.ds(8, own_rows), :] = picked
    edges = [
        remote(csel.at[pl.ds(own_rows - 8, 8)], cext.at[pl.ds(0, 8)], ext_send.at[0], ext_recv.at[0], high_sub),
        remote(csel.at[pl.ds(0, 8)], cext.at[pl.ds(own_rows + 8, 8)], ext_send.at[1], ext_recv.at[1], low_sub),
    ]
    for copy in edges:
        copy.start()

    loading[2].wait()
    ordt[...] = jnp.broadcast_to(ordv[...].astype(F32), (LANES, SUBN)).T

    def numbering(i, carry):
        rows = pl.ds(pl.multiple_of(i * PLANE, PLANE), PLANE)
        odd = lax.rem(i, 2)
        pair = lax.div(i, 2)
        plane = odd * pair + (1 - odd) * (5 - pair)
        hit = iota((PLANE, SUBN), 0) + plane * PLANE == ordv[...]
        permt[rows, :] = jnp.where(hit, 1.0, 0.0).astype(BF16)
        number = ordt[rows, :].astype(jnp.int32)
        for c in range(SUBN // LANES):
            lanes = pl.ds(c * LANES, LANES)
            perm[rows, lanes] = jnp.where(number == iota((PLANE, LANES), 1) + c * LANES, 1.0, 0.0).astype(BF16)
        return carry

    lax.fori_loop(0, 6, numbering, 0)

    def parts(e):
        high, low = split(res[e].reshape(PLANE, LANES))
        rows = pl.ds(pl.multiple_of(e * PLANE, PLANE), PLANE)
        vcat[rows, pl.ds(0, LANES)] = high
        vcat[rows, pl.ds(LANES, LANES)] = low

    def restrict():
        prod = jnp.dot(rmat[...], vcat[...], preferred_element_type=F32)
        prod = prod[:, :LANES] + prod[:, LANES:]
        return prod[0:CV] + prod[CV : 2 * CV]

    def send_all(k, q):
        known[k, s] = q
        with_sub(lambda peer: remote(known.at[k, s], known.at[k, s], one_send.at[k], one_recv.at[k], peer).start())

    loading[0].wait()
    loading[1].wait()
    b_hi, b_lo = split(bas[1])
    rmat[...] = jnp.concatenate([b_hi.astype(F32), b_lo.astype(F32), jnp.zeros((8, SUBN), F32)], axis=0).astype(BF16)
    for e in range(1, 5):
        parts(e)
    halos[0].wait_recv()
    halos[1].wait_recv()
    res[0] = res[0] * m_lo
    res[5] = res[5] * m_hi
    parts(0)
    parts(5)
    send_all(0, restrict())

    sol[...] = jnp.zeros_like(sol)
    csum[...] = jnp.zeros_like(csum)
    loading[5].wait()

    def stencil(src, o, c):
        u = src[o + 1, c].reshape(NB, NB, LANES)
        tx, tr, tc = [int(c == axis) for axis in range(3)]
        below = jnp.concatenate([u[0:1], u[:-1]], axis=0)
        above = jnp.concatenate([u[1:], u[-1:]], axis=0)
        total = diag[o, c].reshape(NB, NB, LANES) * u
        terms = [
            (tx, 0, src[o, c].reshape(NB, NB, LANES)),
            (tx, 1, src[o + 2, c].reshape(NB, NB, LANES)),
            (tr, 2, below),
            (tr, 3, above),
            (tc, 4, pltpu.roll(u, 1, axis=1)),
            (tc, 5, pltpu.roll(u, NB - 1, axis=1)),
        ]
        for kind, way, value in terms:
            total = total - off[o, kind, way].reshape(NB, NB, LANES) * value
        return total.reshape(NODES, LANES)

    def three_parts(x):
        high = x.astype(BF16).astype(F32)
        low = x - high
        return (high + pltpu.roll(low, 16, axis=1) + pltpu.roll(high, 32, axis=1)).astype(BF16)

    def build():
        loading[4].wait()
        loading[8].wait()
        loading[9].wait()
        for copy in halos[2:]:
            copy.wait_recv()
        table[...] = jnp.zeros_like(table)
        for slot, rows, at, mask in ((0, (2, 4), 0, m_lo), (1, (0, 4), 2, None), (2, (0, 2), 6, m_hi)):
            kinds = lab[slot]
            mu = jnp.zeros(kinds.shape, F32)
            pm = jnp.zeros(kinds.shape, F32)
            for r in range(regions):
                mu = jnp.where(kinds == r, shear[r], mu)
                pm = jnp.where(kinds == r, shear[r] * (2.0 + stiff[r]), pm)
            if mask is not None:
                mu, pm = mu * mask, pm * mask
            count = rows[1] - rows[0]
            table[at : at + count, 0:NODES] = mu[rows[0] : rows[1]]
            table[8 + at : 8 + at + count, 0:NODES] = pm[rows[0] : rows[1]]
        turned = table[...].T
        for e in range(8):
            for kind in range(2):
                at = kind * 8 + e
                mods[kind, e] = jnp.broadcast_to(turned[0:NODES, at : at + 1], (NODES, LANES))

        def coefficients(o, carry):
            m_o = jnp.where(o == 0, m_lo, jnp.where(o == 5, m_hi, 1.0))
            m_down = jnp.where(o <= 1, m_lo, m_o)
            m_up = jnp.where(o >= 4, m_hi, m_o)
            row = iota((NB, NB, LANES), 0)
            col = iota((NB, NB, LANES), 1)
            nothing = jnp.zeros((1, NB, LANES), F32)
            sums = []
            for kind in range(2):
                mid = mods[kind, o + 1].reshape(NB, NB, LANES)
                down = 0.25 * (mid + mods[kind, o].reshape(NB, NB, LANES))
                up = 0.25 * (mid + mods[kind, o + 2].reshape(NB, NB, LANES))
                rm = 0.25 * (mid + jnp.concatenate([nothing, mid[:-1]], axis=0))
                rp = 0.25 * (mid + jnp.concatenate([mid[1:], nothing], axis=0))
                cm = 0.25 * (mid + jnp.where(col == 0, 0.0, pltpu.roll(mid, 1, axis=1)))
                cp = 0.25 * (mid + jnp.where(col == NB - 1, 0.0, pltpu.roll(mid, NB - 1, axis=1)))
                sums.append((down + up, rm + rp, cm + cp))
                parts = (
                    down * m_down,
                    up * m_up,
                    jnp.where(row == 0, 0.0, rm) * m_o,
                    jnp.where(row == NB - 1, 0.0, rp) * m_o,
                    jnp.where(col == 0, 0.0, cm) * m_o,
                    jnp.where(col == NB - 1, 0.0, cp) * m_o,
                )
                for way, value in enumerate(parts):
                    off[o, kind, way] = value.reshape(NODES, LANES)
            for c in range(3):
                total = sums[int(c == 0)][0] + sums[int(c == 1)][1] + sums[int(c == 2)][2]
                diag[o, c] = (total * m_o).reshape(NODES, LANES)
            return carry

        lax.fori_loop(0, 6, coefficients, 0)

        xb[...] = jnp.zeros_like(xb)
        xb[0:CV, :] = bas[0] * m_lo
        xb[CV : 2 * CV, :] = bas[1]
        xb[2 * CV : 3 * CV, :] = bas[2] * m_hi
        for c in range(SUBN // LANES):
            xbt[pl.ds(c * LANES, LANES), :] = xb[:, pl.ds(c * LANES, LANES)].T
        lane = lax.div(iota((PLANE, LANES), 1), CV)
        for e in range(8):
            total = jnp.zeros((PLANE, LANES), F32)
            for which, at in ((0, e + 3), (1, e - 1), (2, e - 5)):
                if 0 <= at < 6:
                    total = total + jnp.where(lane == which, xbt[pl.ds(at * PLANE, PLANE), :], 0.0)
            cols[e] = total.reshape(3, NODES, LANES)
            if 2 <= e < 6:
                mpack[pl.ds((e - 2) * PLANE, PLANE), :] = three_parts(total)

        def on_columns(o, carry):
            rows = pl.multiple_of(o * PLANE, PLANE)
            for c in range(3):
                acols[pl.ds(rows + c * NODES, NODES), :] = stencil(cols, o, c)
            apack[pl.ds(rows, PLANE), :] = three_parts(acols[pl.ds(rows, PLANE), :])
            return carry

        lax.fori_loop(0, 6, on_columns, 0)
        a_hi, a_lo = split(acols[...])
        prod = jnp.dot(rmat[...], a_hi, preferred_element_type=F32) + jnp.dot(rmat[...], a_lo, preferred_element_type=F32)
        prod = prod[0:CV] + prod[CV : 2 * CV]
        for i in range(3 * CV):
            bam[i] = jnp.broadcast_to(prod[:, i : i + 1], (CV, LANES))
        cnow[...] = jnp.zeros_like(cnow)

        for copy in edges:
            copy.wait_recv()
        r = iota((groups * 16, own_rows + 16), 0)
        inside = lax.rem(r, 16)
        source = CV + CV * lax.div(r, 16) + inside
        take = jnp.where((iota((groups * 16, own_rows + 16), 1) == source) & (inside < 3 * CV), 1.0, 0.0).astype(BF16)
        e_hi, e_lo = split(cext[...])
        w_hi = jnp.dot(take, e_hi, preferred_element_type=F32).astype(BF16)
        w_lo = jnp.dot(take, e_lo, preferred_element_type=F32).astype(BF16)
        cbig[:, pl.ds(0, width)] = w_hi
        cbig[:, pl.ds(width, width)] = w_lo
        cbig[:, pl.ds(2 * width, width)] = w_hi

    def spread(c):
        c_hi = c.astype(BF16)
        c_lo = (c - c_hi.astype(F32)).astype(BF16)
        return jnp.concatenate([c_hi, c_hi, c_lo, jnp.zeros((LANES - 48, LANES), BF16)], axis=0)

    def iteration(k, carry):
        pv[...] = jnp.dot(perm[...], vcat[:, pl.ds(0, LANES)], preferred_element_type=F32).astype(BF16)
        high, low = split(jnp.dot(inv[...], pv[...], preferred_element_type=F32))
        ycat[:, pl.ds(0, LANES)] = high
        ycat[:, pl.ds(LANES, LANES)] = low

        def swap(e, there, slot, peer, way):
            remote(yown.at[k, e], there.at[k, slot], y_send.at[way, k], y_recv.at[way, k], peer).start()

        for pair in range(3):
            high, low = 5 - pair, pair
            rows = pl.ds(2 * pair * PLANE, 2 * PLANE)
            back = jnp.dot(permt[rows, :], ycat[...], preferred_element_type=F32)
            back = (back[:, :LANES] + back[:, LANES:]).reshape(2, 3, NODES, LANES)
            yown[k, high] = back[0]
            yown[k, low] = back[1]
            swap(high, yleft, 2 - pair, right, 2 * pair)
            swap(low, yright, pair, left, 2 * pair + 1)

        pl.when(k == 0)(build)

        wait_for(known.at[k, pl.ds(0, subs - 1)], one_recv.at[k])
        gathered = known[k].reshape(width, LANES)
        q_hi, q_lo = split(gathered)
        mixed = jnp.concatenate([q_hi, q_hi, q_lo], axis=0)
        part[k] = jnp.dot(cbig[...], mixed, preferred_element_type=F32).reshape(groups, 16, LANES)
        for d in gsteps:
            o = group_peer(d)
            remote(part.at[k, o], arrive.at[k, g], thr_send.at[k], thr_recv.at[k], {"sub": s, "grp": o}).start()
        arrive[k, g] = part[k, g]

        for way, ref in ((0, yleft.at[k, 2]), (1, yright.at[k, 0]), (2, yleft.at[k, 1]), (3, yright.at[k, 1])):
            wait_for(ref, y_recv.at[way, k])
        zbuf[1] = yleft[k, 1] + yown[k, 0]
        zbuf[2] = yleft[k, 2] * m_lo + yown[k, 1]
        zbuf[3] = yown[k, 2]
        zbuf[4] = yown[k, 3]
        zbuf[5] = yown[k, 4] + yright[k, 0] * m_hi
        zbuf[6] = yown[k, 5] + yright[k, 1]
        for e in range(4):
            sol[e] = sol[e] + 0.5 * zbuf[e + 2]

        def update(o, carry):
            for c in range(3):
                res[o, c] = res[o, c] - stencil(zbuf, o, c)
            parts(o)
            return carry

        lax.fori_loop(1, 5, update, 0)
        wait_for(yleft.at[k, 0], y_recv.at[4, k])
        wait_for(yright.at[k, 2], y_recv.at[5, k])
        zbuf[0] = yleft[k, 0]
        zbuf[7] = yright[k, 2]
        update(0, 0)
        update(5, 0)

        @pl.when(k < ITERS - 1)
        def _():
            qnext[...] = restrict()

        wait_for(arrive.at[k, pl.ds(0, groups - 1)], thr_recv.at[k])
        c = jnp.sum(arrive[k], axis=0)
        cnow[...] = c
        csum[...] = csum[...] + c

        @pl.when(k < ITERS - 1)
        def _():
            q = qnext[...]
            for i in range(3 * CV):
                q = q - bam[i] * jnp.broadcast_to(cnow[i : i + 1, :], (CV, LANES))
            send_all(k + 1, q)

        weights = spread(c)
        for e in range(6):
            change = jnp.dot(apack[pl.ds(e * PLANE, PLANE), :], weights, preferred_element_type=F32)
            now = res[e].reshape(PLANE, LANES) - change
            res[e] = now.reshape(3, NODES, LANES)
            vcat[pl.ds(e * PLANE, PLANE), pl.ds(0, LANES)] = now.astype(BF16)
        return carry

    lax.fori_loop(0, ITERS, iteration, 0)

    weights = spread(csum[...])
    for e in range(4):
        change = jnp.dot(mpack[pl.ds(e * PLANE, PLANE), :], weights, preferred_element_type=F32)
        sol_out[e] = sol[e] + 0.5 * change.reshape(3, NODES, LANES)
        res_out[e] = res[e + 1]
    cv_out[...] = cnow[CV : 2 * CV, :]

    for copy in halos + edges:
        copy.wait_send()
    for k in range(ITERS):
        wait_for(known.at[k, pl.ds(0, subs - 1)], one_send.at[k])
        wait_for(arrive.at[k, pl.ds(0, groups - 1)], thr_send.at[k])
        for way in range(6):
            wait_for(yleft.at[k, 0], y_send.at[way, k])


def deliver(sol_in, res_in, cv_in, sol_out, res_out, cv_out, sem):
    copies = [
        pltpu.make_async_copy(sol_in, sol_out, sem.at[0]),
        pltpu.make_async_copy(res_in, res_out, sem.at[1]),
        pltpu.make_async_copy(cv_in, cv_out, sem.at[2]),
    ]
    for copy in copies:
        copy.start()
    for copy in copies:
        copy.wait()


def body(side, groups, loads, labels, shear, stiff, order, inverse, basis, coarse):
    planes = loads.shape[0]
    regions = shear.shape[0]
    span = coarse.shape[1]
    width = side * side * CV
    own_rows = groups * CV
    plane = (3, NODES, LANES)
    dma = pltpu.SemaphoreType.DMA
    anywhere = pl.BlockSpec(memory_space=pl.ANY)
    inside = pl.BlockSpec(memory_space=pltpu.VMEM)
    scratch = [
        pltpu.VMEM((16, SUBN), BF16),
        pltpu.VMEM((2, *plane), F32),
        pltpu.SMEM((regions,), F32),
        pltpu.SMEM((regions,), F32),
        pltpu.VMEM((6, *plane), F32),
        pltpu.VMEM((4, *plane), F32),
        pltpu.VMEM((8, *plane), F32),
        pltpu.VMEM((SUBN, 2 * LANES), BF16),
        pltpu.VMEM((SUBN, LANES), BF16),
        pltpu.VMEM((SUBN, 2 * LANES), BF16),
        pltpu.VMEM((ITERS, 6, *plane), F32),
        pltpu.VMEM((ITERS, 3, *plane), F32),
        pltpu.VMEM((ITERS, 3, *plane), F32),
        pltpu.VMEM((SUBN, SUBN), BF16),
        pltpu.VMEM((SUBN, SUBN), BF16),
        pltpu.VMEM((SUBN, SUBN), BF16),
        pltpu.VMEM((1, SUBN), jnp.int32),
        pltpu.VMEM((SUBN, LANES), F32),
        pltpu.VMEM((3, 4, NODES), jnp.int32),
        pltpu.VMEM((3, CV, SUBN), F32),
        pltpu.VMEM((own_rows, span), F32),
        pltpu.VMEM((own_rows, width), F32),
        pltpu.VMEM((own_rows + 16, width), F32),
        pltpu.VMEM((groups * 16, 3 * width), BF16),
        pltpu.VMEM((ITERS, side * side, CV, LANES), F32),
        pltpu.VMEM((ITERS, groups, 16, LANES), F32),
        pltpu.VMEM((ITERS, groups, 16, LANES), F32),
        pltpu.VMEM((LANES, LANES), F32),
        pltpu.VMEM((2, 8, NODES, LANES), F32),
        pltpu.VMEM((6, 2, 6, NODES, LANES), F32),
        pltpu.VMEM((6, *plane), F32),
        pltpu.VMEM((LANES, SUBN), F32),
        pltpu.VMEM((SUBN, LANES), F32),
        pltpu.VMEM((8, *plane), F32),
        pltpu.VMEM((SUBN, LANES), F32),
        pltpu.VMEM((4 * PLANE, LANES), BF16),
        pltpu.VMEM((SUBN, LANES), BF16),
        pltpu.VMEM((3 * CV, CV, LANES), F32),
        pltpu.VMEM((CV, LANES), F32),
        pltpu.VMEM((16, LANES), F32),
        pltpu.VMEM((16, LANES), F32),
        dma((10,)),
        dma((6,)),
        dma((6,)),
        dma((2,)),
        dma((2,)),
        dma((ITERS,)),
        dma((ITERS,)),
        dma((ITERS,)),
        dma((ITERS,)),
        dma((6, ITERS)),
        dma((6, ITERS)),
    ]
    outs = (
        jax.ShapeDtypeStruct((planes, *plane), F32),
        jax.ShapeDtypeStruct((planes, *plane), F32),
        jax.ShapeDtypeStruct((CV, LANES), F32),
    )
    held = pl.pallas_call(
        functools.partial(kernel, side, groups, regions),
        out_shape=(
            pltpu.VMEM((planes, *plane), F32),
            pltpu.VMEM((planes, *plane), F32),
            pltpu.VMEM((CV, LANES), F32),
        ),
        in_specs=[anywhere, anywhere, anywhere, anywhere, anywhere, anywhere, anywhere, anywhere],
        out_specs=(inside, inside, inside),
        scratch_shapes=scratch,
        compiler_params=pltpu.CompilerParams(collective_id=0, has_side_effects=True),
        name="schwarz",
    )(loads, labels, shear, stiff, order, inverse, basis, coarse)
    return pl.pallas_call(
        deliver,
        out_shape=outs,
        in_specs=[anywhere] * 3,
        out_specs=(anywhere,) * 3,
        scratch_shapes=[dma((3,))],
        compiler_params=pltpu.CompilerParams(vmem_limit_bytes=1 << 20),
        name="deliver",
    )(*held)


def solution(mesh):
    subs, groups = mesh.shape["sub"], mesh.shape["grp"]
    side = round(subs**0.5)
    chain = ("sub", "grp")
    return jax.shard_map(
        functools.partial(body, side, groups),
        mesh=mesh,
        in_specs=(
            P(chain, None, None, None),
            P(chain, None),
            P(),
            P(),
            P(chain, None),
            P(chain, None, None),
            P(chain, None, None),
            P("sub", None),
        ),
        out_specs=(P(chain, None, None, None), P(chain, None, None, None), P(chain, None)),
        check_vma=False,
    )
```

```python
import functools

import jax
import jax.numpy as jnp
from jax import lax
from jax.experimental import pallas as pl
from jax.experimental.pallas import tpu as pltpu
from jax.sharding import PartitionSpec as P

ITERS = 3
NODES = 64
NB = 8
CV = 4
SUBN = 1152
LANES = 128
PLANE = 3 * NODES
MESH = pl.DeviceIdType.MESH
F32 = jnp.float32
BF16 = jnp.bfloat16


def wait_for(ref, sem):
    pltpu.make_async_copy(ref, ref, sem).wait()


def iota(shape, axis):
    return lax.broadcasted_iota(jnp.int32, shape, axis)


def split(x):
    high = x.astype(BF16)
    return high, (x - high.astype(F32)).astype(BF16)


def kernel(
    side,
    groups,
    regions,
    loads,
    labels,
    shear_in,
    stiff_in,
    order,
    inverse,
    basis,
    coarse,
    sol_out,
    res_out,
    cv_out,
    rmat,
    edge,
    shear,
    stiff,
    res,
    sol,
    zbuf,
    vcat,
    pv,
    ycat,
    yown,
    yleft,
    yright,
    perm,
    permt,
    inv,
    ordv,
    ordt,
    lab,
    bas,
    crs,
    csel,
    cext,
    cbig,
    known,
    part,
    arrive,
    table,
    mods,
    off,
    diag,
    xb,
    xbt,
    cols,
    acols,
    mpack,
    apack,
    bam,
    qnext,
    cnow,
    csum,
    load_sem,
    halo_send,
    halo_recv,
    ext_send,
    ext_recv,
    one_send,
    one_recv,
    thr_send,
    thr_recv,
    y_send,
    y_recv,
):
    subs = side * side
    chain = subs * groups
    s = lax.axis_index("sub")
    g = lax.axis_index("grp")
    z = lax.div(s, side)
    y = lax.rem(s, side)
    here = s * groups + g
    before = lax.rem(here + chain - 1, chain)
    after = lax.rem(here + 1, chain)
    left = {"sub": lax.div(before, groups), "grp": lax.rem(before, groups)}
    right = {"sub": lax.div(after, groups), "grp": lax.rem(after, groups)}
    low_sub = {"sub": lax.rem(s + subs - 1, subs), "grp": g}
    high_sub = {"sub": lax.rem(s + 1, subs), "grp": g}
    m_lo = jnp.where(here == 0, 0.0, 1.0).astype(F32)
    m_hi = jnp.where(here == chain - 1, 0.0, 1.0).astype(F32)

    gsteps = sorted(range(1, groups), key=lambda d: -min(d, groups - d))

    half = side // 2
    skip = half * side + half

    def far_first(i):
        oz = lax.rem(z + half + lax.div(i, side), side)
        oy = lax.rem(y + half + lax.rem(i, side), side)
        return {"sub": oz * side + oy, "grp": g}

    def with_sub(visit):
        def step(i, carry):
            visit(far_first(i))
            return carry

        for i in range(subs):
            if i != skip:
                step(i, 0)

    def group_peer(d):
        return lax.rem(g + d, groups)

    def local(src, dst, at):
        return pltpu.make_async_copy(src, dst, load_sem.at[at])

    loading = [
        local(loads, res.at[pl.ds(1, 4)], 0),
        local(basis.at[0], bas.at[1], 1),
        local(order, ordv, 2),
        local(coarse, crs, 3),
        local(labels, lab.at[1], 4),
        local(inverse.at[0], inv, 5),
        local(loads.at[3], edge.at[0], 6),
        local(loads.at[0], edge.at[1], 7),
        local(shear_in, shear, 8),
        local(stiff_in, stiff, 9),
    ]
    for at in (6, 7, 0, 1, 2, 3, 4, 8, 9, 5):
        loading[at].start()

    barrier = pltpu.get_barrier_semaphore()
    peers = [left, right] + [{"sub": s, "grp": group_peer(d)} for d in gsteps]
    for peer in peers:
        pl.semaphore_signal(barrier, inc=1, device_id=peer, device_id_type=MESH)
    with_sub(lambda peer: pl.semaphore_signal(barrier, inc=1, device_id=peer, device_id_type=MESH))
    pl.semaphore_wait(barrier, len(peers) + subs - 1)

    def remote(src, dst, send, recv, peer):
        return pltpu.make_async_remote_copy(
            src_ref=src, dst_ref=dst, send_sem=send, recv_sem=recv, device_id=peer, device_id_type=MESH
        )

    loading[6].wait()
    loading[7].wait()
    halos = [
        remote(edge.at[0], res.at[0], halo_send.at[0], halo_recv.at[0], right),
        remote(edge.at[1], res.at[5], halo_send.at[1], halo_recv.at[1], left),
        remote(basis.at[0], bas.at[0], halo_send.at[2], halo_recv.at[2], right),
        remote(basis.at[0], bas.at[2], halo_send.at[3], halo_recv.at[3], left),
        remote(labels, lab.at[0], halo_send.at[4], halo_recv.at[4], right),
        remote(labels, lab.at[2], halo_send.at[5], halo_recv.at[5], left),
    ]
    for copy in halos:
        copy.start()

    loading[3].wait()
    width = subs * CV
    place = iota((1, width), 1)
    wanted = (lax.div(place, CV) * groups + g) * CV + lax.rem(place, CV)
    span = crs.shape[1]
    choose = jnp.where(iota((span, width), 0) == wanted, 1.0, 0.0).astype(BF16)
    c_hi, c_lo = split(crs[...])
    picked = jnp.dot(c_hi, choose, preferred_element_type=F32) + jnp.dot(c_lo, choose, preferred_element_type=F32)
    own_rows = groups * CV
    csel[...] = picked
    cext[pl.ds(8, own_rows), :] = picked
    edges = [
        remote(csel.at[pl.ds(own_rows - 8, 8)], cext.at[pl.ds(0, 8)], ext_send.at[0], ext_recv.at[0], high_sub),
        remote(csel.at[pl.ds(0, 8)], cext.at[pl.ds(own_rows + 8, 8)], ext_send.at[1], ext_recv.at[1], low_sub),
    ]
    for copy in edges:
        copy.start()

    loading[2].wait()
    ordt[...] = jnp.broadcast_to(ordv[...].astype(F32), (LANES, SUBN)).T

    def numbering(i, carry):
        rows = pl.ds(pl.multiple_of(i * PLANE, PLANE), PLANE)
        odd = lax.rem(i, 2)
        pair = lax.div(i, 2)
        plane = odd * pair + (1 - odd) * (5 - pair)
        hit = iota((PLANE, SUBN), 0) + plane * PLANE == ordv[...]
        permt[rows, :] = jnp.where(hit, 1.0, 0.0).astype(BF16)
        number = ordt[rows, :].astype(jnp.int32)
        for c in range(SUBN // LANES):
            lanes = pl.ds(c * LANES, LANES)
            perm[rows, lanes] = jnp.where(number == iota((PLANE, LANES), 1) + c * LANES, 1.0, 0.0).astype(BF16)
        return carry

    lax.fori_loop(0, 6, numbering, 0)

    def parts(e):
        high, low = split(res[e].reshape(PLANE, LANES))
        rows = pl.ds(pl.multiple_of(e * PLANE, PLANE), PLANE)
        vcat[rows, pl.ds(0, LANES)] = high
        vcat[rows, pl.ds(LANES, LANES)] = low

    def restrict():
        prod = jnp.dot(rmat[...], vcat[...], preferred_element_type=F32)
        prod = prod[:, :LANES] + prod[:, LANES:]
        return prod[0:CV] + prod[CV : 2 * CV]

    def send_all(k, q):
        known[k, s] = q
        with_sub(lambda peer: remote(known.at[k, s], known.at[k, s], one_send.at[k], one_recv.at[k], peer).start())

    loading[0].wait()
    loading[1].wait()
    b_hi, b_lo = split(bas[1])
    rmat[...] = jnp.concatenate([b_hi.astype(F32), b_lo.astype(F32), jnp.zeros((8, SUBN), F32)], axis=0).astype(BF16)
    for e in range(1, 5):
        parts(e)
    halos[0].wait_recv()
    halos[1].wait_recv()
    res[0] = res[0] * m_lo
    res[5] = res[5] * m_hi
    parts(0)
    parts(5)
    send_all(0, restrict())

    sol[...] = jnp.zeros_like(sol)
    csum[...] = jnp.zeros_like(csum)
    loading[5].wait()

    def stencil(src, o, c):
        u = src[o + 1, c].reshape(NB, NB, LANES)
        tx, tr, tc = [int(c == axis) for axis in range(3)]
        below = jnp.concatenate([u[0:1], u[:-1]], axis=0)
        above = jnp.concatenate([u[1:], u[-1:]], axis=0)
        total = diag[o, c].reshape(NB, NB, LANES) * u
        terms = [
            (tx, 0, src[o, c].reshape(NB, NB, LANES)),
            (tx, 1, src[o + 2, c].reshape(NB, NB, LANES)),
            (tr, 2, below),
            (tr, 3, above),
            (tc, 4, pltpu.roll(u, 1, axis=1)),
            (tc, 5, pltpu.roll(u, NB - 1, axis=1)),
        ]
        for kind, way, value in terms:
            total = total - off[o, kind, way].reshape(NB, NB, LANES) * value
        return total.reshape(NODES, LANES)

    def three_parts(x):
        high = x.astype(BF16).astype(F32)
        low = x - high
        return (high + pltpu.roll(low, 16, axis=1) + pltpu.roll(high, 32, axis=1)).astype(BF16)

    def build():
        loading[4].wait()
        loading[8].wait()
        loading[9].wait()
        for copy in halos[2:]:
            copy.wait_recv()
        table[...] = jnp.zeros_like(table)
        for slot, rows, at, mask in ((0, (2, 4), 0, m_lo), (1, (0, 4), 2, None), (2, (0, 2), 6, m_hi)):
            kinds = lab[slot]
            mu = jnp.zeros(kinds.shape, F32)
            pm = jnp.zeros(kinds.shape, F32)
            for r in range(regions):
                mu = jnp.where(kinds == r, shear[r], mu)
                pm = jnp.where(kinds == r, shear[r] * (2.0 + stiff[r]), pm)
            if mask is not None:
                mu, pm = mu * mask, pm * mask
            count = rows[1] - rows[0]
            table[at : at + count, 0:NODES] = mu[rows[0] : rows[1]]
            table[8 + at : 8 + at + count, 0:NODES] = pm[rows[0] : rows[1]]
        turned = table[...].T
        for e in range(8):
            for kind in range(2):
                at = kind * 8 + e
                mods[kind, e] = jnp.broadcast_to(turned[0:NODES, at : at + 1], (NODES, LANES))

        def coefficients(o, carry):
            m_o = jnp.where(o == 0, m_lo, jnp.where(o == 5, m_hi, 1.0))
            m_down = jnp.where(o <= 1, m_lo, m_o)
            m_up = jnp.where(o >= 4, m_hi, m_o)
            row = iota((NB, NB, LANES), 0)
            col = iota((NB, NB, LANES), 1)
            nothing = jnp.zeros((1, NB, LANES), F32)
            sums = []
            for kind in range(2):
                mid = mods[kind, o + 1].reshape(NB, NB, LANES)
                down = 0.25 * (mid + mods[kind, o].reshape(NB, NB, LANES))
                up = 0.25 * (mid + mods[kind, o + 2].reshape(NB, NB, LANES))
                rm = 0.25 * (mid + jnp.concatenate([nothing, mid[:-1]], axis=0))
                rp = 0.25 * (mid + jnp.concatenate([mid[1:], nothing], axis=0))
                cm = 0.25 * (mid + jnp.where(col == 0, 0.0, pltpu.roll(mid, 1, axis=1)))
                cp = 0.25 * (mid + jnp.where(col == NB - 1, 0.0, pltpu.roll(mid, NB - 1, axis=1)))
                sums.append((down + up, rm + rp, cm + cp))
                parts = (
                    down * m_down,
                    up * m_up,
                    jnp.where(row == 0, 0.0, rm) * m_o,
                    jnp.where(row == NB - 1, 0.0, rp) * m_o,
                    jnp.where(col == 0, 0.0, cm) * m_o,
                    jnp.where(col == NB - 1, 0.0, cp) * m_o,
                )
                for way, value in enumerate(parts):
                    off[o, kind, way] = value.reshape(NODES, LANES)
            for c in range(3):
                total = sums[int(c == 0)][0] + sums[int(c == 1)][1] + sums[int(c == 2)][2]
                diag[o, c] = (total * m_o).reshape(NODES, LANES)
            return carry

        lax.fori_loop(0, 6, coefficients, 0)

        xb[...] = jnp.zeros_like(xb)
        xb[0:CV, :] = bas[0] * m_lo
        xb[CV : 2 * CV, :] = bas[1]
        xb[2 * CV : 3 * CV, :] = bas[2] * m_hi
        for c in range(SUBN // LANES):
            xbt[pl.ds(c * LANES, LANES), :] = xb[:, pl.ds(c * LANES, LANES)].T
        lane = lax.div(iota((PLANE, LANES), 1), CV)
        for e in range(8):
            total = jnp.zeros((PLANE, LANES), F32)
            for which, at in ((0, e + 3), (1, e - 1), (2, e - 5)):
                if 0 <= at < 6:
                    total = total + jnp.where(lane == which, xbt[pl.ds(at * PLANE, PLANE), :], 0.0)
            cols[e] = total.reshape(3, NODES, LANES)
            if 2 <= e < 6:
                mpack[pl.ds((e - 2) * PLANE, PLANE), :] = three_parts(total)

        def on_columns(o, carry):
            rows = pl.multiple_of(o * PLANE, PLANE)
            for c in range(3):
                acols[pl.ds(rows + c * NODES, NODES), :] = stencil(cols, o, c)
            apack[pl.ds(rows, PLANE), :] = three_parts(acols[pl.ds(rows, PLANE), :])
            return carry

        lax.fori_loop(0, 6, on_columns, 0)
        a_hi, a_lo = split(acols[...])
        prod = jnp.dot(rmat[...], a_hi, preferred_element_type=F32) + jnp.dot(rmat[...], a_lo, preferred_element_type=F32)
        prod = prod[0:CV] + prod[CV : 2 * CV]
        for i in range(3 * CV):
            bam[i] = jnp.broadcast_to(prod[:, i : i + 1], (CV, LANES))
        cnow[...] = jnp.zeros_like(cnow)

        for copy in edges:
            copy.wait_recv()
        r = iota((groups * 16, own_rows + 16), 0)
        inside = lax.rem(r, 16)
        source = CV + CV * lax.div(r, 16) + inside
        take = jnp.where((iota((groups * 16, own_rows + 16), 1) == source) & (inside < 3 * CV), 1.0, 0.0).astype(BF16)
        e_hi, e_lo = split(cext[...])
        w_hi = jnp.dot(take, e_hi, preferred_element_type=F32).astype(BF16)
        w_lo = jnp.dot(take, e_lo, preferred_element_type=F32).astype(BF16)
        cbig[pl.ds(0, groups * 16), :] = w_hi
        cbig[pl.ds(groups * 16, groups * 16), :] = w_lo

    def spread(c):
        c_hi = c.astype(BF16)
        c_lo = (c - c_hi.astype(F32)).astype(BF16)
        return jnp.concatenate([c_hi, c_hi, c_lo, jnp.zeros((LANES - 48, LANES), BF16)], axis=0)

    def iteration(k, carry):
        pv[...] = jnp.dot(perm[...], vcat[:, pl.ds(0, LANES)], preferred_element_type=F32).astype(BF16)
        high, low = split(jnp.dot(inv[...], pv[...], preferred_element_type=F32))
        ycat[:, pl.ds(0, LANES)] = high
        ycat[:, pl.ds(LANES, LANES)] = low

        def swap(e, there, slot, peer, way):
            remote(yown.at[k, e], there.at[k, slot], y_send.at[way, k], y_recv.at[way, k], peer).start()

        for pair in range(3):
            high, low = 5 - pair, pair
            rows = pl.ds(2 * pair * PLANE, 2 * PLANE)
            back = jnp.dot(permt[rows, :], ycat[...], preferred_element_type=F32)
            back = (back[:, :LANES] + back[:, LANES:]).reshape(2, 3, NODES, LANES)
            yown[k, high] = back[0]
            yown[k, low] = back[1]
            swap(high, yleft, 2 - pair, right, 2 * pair)
            swap(low, yright, pair, left, 2 * pair + 1)

        pl.when(k == 0)(build)

        wait_for(known.at[k, pl.ds(0, subs - 1)], one_recv.at[k])
        gathered = known[k].reshape(width, LANES)
        q_hi, q_lo = split(gathered)
        main = jnp.dot(cbig[...], q_hi, preferred_element_type=F32)
        rest = jnp.dot(cbig[pl.ds(0, groups * 16), :], q_lo, preferred_element_type=F32)
        part[k] = (main[: groups * 16] + (main[groups * 16 :] + rest)).reshape(groups, 16, LANES)
        for d in gsteps:
            o = group_peer(d)
            remote(part.at[k, o], arrive.at[k, g], thr_send.at[k], thr_recv.at[k], {"sub": s, "grp": o}).start()
        arrive[k, g] = part[k, g]

        for way, ref in ((0, yleft.at[k, 2]), (1, yright.at[k, 0]), (2, yleft.at[k, 1]), (3, yright.at[k, 1])):
            wait_for(ref, y_recv.at[way, k])
        zbuf[1] = yleft[k, 1] + yown[k, 0]
        zbuf[2] = yleft[k, 2] * m_lo + yown[k, 1]
        zbuf[3] = yown[k, 2]
        zbuf[4] = yown[k, 3]
        zbuf[5] = yown[k, 4] + yright[k, 0] * m_hi
        zbuf[6] = yown[k, 5] + yright[k, 1]
        for e in range(4):
            sol[e] = sol[e] + 0.5 * zbuf[e + 2]

        def update(o, carry):
            for c in range(3):
                res[o, c] = res[o, c] - stencil(zbuf, o, c)
            parts(o)
            return carry

        lax.fori_loop(1, 5, update, 0)
        wait_for(yleft.at[k, 0], y_recv.at[4, k])
        wait_for(yright.at[k, 2], y_recv.at[5, k])
        zbuf[0] = yleft[k, 0]
        zbuf[7] = yright[k, 2]
        update(0, 0)
        update(5, 0)

        @pl.when(k < ITERS - 1)
        def _():
            qnext[...] = restrict()

        wait_for(arrive.at[k, pl.ds(0, groups - 1)], thr_recv.at[k])
        c = jnp.sum(arrive[k], axis=0)
        cnow[...] = c
        csum[...] = csum[...] + c

        @pl.when(k < ITERS - 1)
        def _():
            q = qnext[...]
            for i in range(3 * CV):
                q = q - bam[i] * jnp.broadcast_to(cnow[i : i + 1, :], (CV, LANES))
            send_all(k + 1, q)

        @pl.when(k < ITERS - 1)
        def _():
            weights = spread(c)
            for e in range(6):
                change = jnp.dot(apack[pl.ds(e * PLANE, PLANE), :], weights, preferred_element_type=F32)
                now = res[e].reshape(PLANE, LANES) - change
                res[e] = now.reshape(3, NODES, LANES)
                vcat[pl.ds(e * PLANE, PLANE), pl.ds(0, LANES)] = now.astype(BF16)

        return carry

    lax.fori_loop(0, ITERS, iteration, 0)

    weights = spread(csum[...])
    latest = spread(cnow[...])
    for e in range(4):
        final = jnp.dot(apack[pl.ds((e + 1) * PLANE, PLANE), :], latest, preferred_element_type=F32)
        res_out[e] = res[e + 1] - final.reshape(3, NODES, LANES)
        change = jnp.dot(mpack[pl.ds(e * PLANE, PLANE), :], weights, preferred_element_type=F32)
        sol_out[e] = sol[e] + 0.5 * change.reshape(3, NODES, LANES)
    cv_out[...] = cnow[CV : 2 * CV, :]

    for copy in halos + edges:
        copy.wait_send()
    for k in range(ITERS):
        wait_for(known.at[k, pl.ds(0, subs - 1)], one_send.at[k])
        wait_for(arrive.at[k, pl.ds(0, groups - 1)], thr_send.at[k])
        for way in range(6):
            wait_for(yleft.at[k, 0], y_send.at[way, k])


def deliver(sol_in, res_in, cv_in, sol_out, res_out, cv_out, sem):
    copies = [
        pltpu.make_async_copy(sol_in, sol_out, sem.at[0]),
        pltpu.make_async_copy(res_in, res_out, sem.at[1]),
        pltpu.make_async_copy(cv_in, cv_out, sem.at[2]),
    ]
    for copy in copies:
        copy.start()
    for copy in copies:
        copy.wait()


def body(side, groups, loads, labels, shear, stiff, order, inverse, basis, coarse):
    planes = loads.shape[0]
    regions = shear.shape[0]
    span = coarse.shape[1]
    width = side * side * CV
    own_rows = groups * CV
    plane = (3, NODES, LANES)
    dma = pltpu.SemaphoreType.DMA
    anywhere = pl.BlockSpec(memory_space=pl.ANY)
    inside = pl.BlockSpec(memory_space=pltpu.VMEM)
    scratch = [
        pltpu.VMEM((16, SUBN), BF16),
        pltpu.VMEM((2, *plane), F32),
        pltpu.SMEM((regions,), F32),
        pltpu.SMEM((regions,), F32),
        pltpu.VMEM((6, *plane), F32),
        pltpu.VMEM((4, *plane), F32),
        pltpu.VMEM((8, *plane), F32),
        pltpu.VMEM((SUBN, 2 * LANES), BF16),
        pltpu.VMEM((SUBN, LANES), BF16),
        pltpu.VMEM((SUBN, 2 * LANES), BF16),
        pltpu.VMEM((ITERS, 6, *plane), F32),
        pltpu.VMEM((ITERS, 3, *plane), F32),
        pltpu.VMEM((ITERS, 3, *plane), F32),
        pltpu.VMEM((SUBN, SUBN), BF16),
        pltpu.VMEM((SUBN, SUBN), BF16),
        pltpu.VMEM((SUBN, SUBN), BF16),
        pltpu.VMEM((1, SUBN), jnp.int32),
        pltpu.VMEM((SUBN, LANES), F32),
        pltpu.VMEM((3, 4, NODES), jnp.int32),
        pltpu.VMEM((3, CV, SUBN), F32),
        pltpu.VMEM((own_rows, span), F32),
        pltpu.VMEM((own_rows, width), F32),
        pltpu.VMEM((own_rows + 16, width), F32),
        pltpu.VMEM((groups * 32, width), BF16),
        pltpu.VMEM((ITERS, side * side, CV, LANES), F32),
        pltpu.VMEM((ITERS, groups, 16, LANES), F32),
        pltpu.VMEM((ITERS, groups, 16, LANES), F32),
        pltpu.VMEM((LANES, LANES), F32),
        pltpu.VMEM((2, 8, NODES, LANES), F32),
        pltpu.VMEM((6, 2, 6, NODES, LANES), F32),
        pltpu.VMEM((6, *plane), F32),
        pltpu.VMEM((LANES, SUBN), F32),
        pltpu.VMEM((SUBN, LANES), F32),
        pltpu.VMEM((8, *plane), F32),
        pltpu.VMEM((SUBN, LANES), F32),
        pltpu.VMEM((4 * PLANE, LANES), BF16),
        pltpu.VMEM((SUBN, LANES), BF16),
        pltpu.VMEM((3 * CV, CV, LANES), F32),
        pltpu.VMEM((CV, LANES), F32),
        pltpu.VMEM((16, LANES), F32),
        pltpu.VMEM((16, LANES), F32),
        dma((10,)),
        dma((6,)),
        dma((6,)),
        dma((2,)),
        dma((2,)),
        dma((ITERS,)),
        dma((ITERS,)),
        dma((ITERS,)),
        dma((ITERS,)),
        dma((6, ITERS)),
        dma((6, ITERS)),
    ]
    outs = (
        jax.ShapeDtypeStruct((planes, *plane), F32),
        jax.ShapeDtypeStruct((planes, *plane), F32),
        jax.ShapeDtypeStruct((CV, LANES), F32),
    )
    held = pl.pallas_call(
        functools.partial(kernel, side, groups, regions),
        out_shape=(
            pltpu.VMEM((planes, *plane), F32),
            pltpu.VMEM((planes, *plane), F32),
            pltpu.VMEM((CV, LANES), F32),
        ),
        in_specs=[anywhere, anywhere, anywhere, anywhere, anywhere, anywhere, anywhere, anywhere],
        out_specs=(inside, inside, inside),
        scratch_shapes=scratch,
        compiler_params=pltpu.CompilerParams(collective_id=0, has_side_effects=True),
        name="schwarz",
    )(loads, labels, shear, stiff, order, inverse, basis, coarse)
    return pl.pallas_call(
        deliver,
        out_shape=outs,
        in_specs=[anywhere] * 3,
        out_specs=(anywhere,) * 3,
        scratch_shapes=[dma((3,))],
        compiler_params=pltpu.CompilerParams(vmem_limit_bytes=1 << 20),
        name="deliver",
    )(*held)


def solution(mesh):
    subs, groups = mesh.shape["sub"], mesh.shape["grp"]
    side = round(subs**0.5)
    chain = ("sub", "grp")
    return jax.shard_map(
        functools.partial(body, side, groups),
        mesh=mesh,
        in_specs=(
            P(chain, None, None, None),
            P(chain, None),
            P(),
            P(),
            P(chain, None),
            P(chain, None, None),
            P(chain, None, None),
            P("sub", None),
        ),
        out_specs=(P(chain, None, None, None), P(chain, None, None, None), P(chain, None)),
        check_vma=False,
    )
```
